32 devices in a mesh: row: 8 (over z, y), col: 4 (over x, core).
Axes of the slice: x: 2, y: 2, z: 4, core: 2. Of those that a mesh axis runs over, the one named last changes fastest.
Arguments:
- front: bfloat16 [8192, 8192], P('row', 'col'), may hold values from -0.125 to 0.125
- tile_mask: int32 [32, 32], P('row', 'col'), may hold values 0 or 1
- probes: bfloat16 [8192, 256], P(('col', 'row')), may hold values from -6 to 6
- coupling: float32 [8192, 256], P(('row', 'col')), may hold values from -0.375 to 0.375
Outputs:
- leaf_basis: float32 [8192, 256], P(('row', 'col'))
- upper_transfer: float32 [4, 8192, 256], P(None, ('row', 'col'))
The draws below stay inside these ranges and needn't reach their ends.
Inputs may be any that keep to these rules, and one draw needn't show every extreme that they name: `tile_mask`: 1 where a tile of the front is present, 0 where it is absent.
All inputs are finite; a program needn't handle non-finite values. No bound on the sum of `tile_mask` on one device may be relied on, other than what follows from the above.
Results may differ from the reference program's by a relative error of at most 0.0003.
Values may be sent and summed in bfloat16 or wider, within the bound.
No kernel may reach another device: no remote copies, remote signals or barrier semaphores. Data moves between devices by JAX's collectives and lax.ppermute only.
A program may use at most 128 MiB of HBM per device.

```python
import jax
import jax.numpy as jnp
from jax import lax

LEAF = 256
PROBES = 256
LEAVES = 32
FRONT = 8192
LEVELS = 5


def place_ends(entries, own_key, least, largest):
    place = [jax.random.randint(jax.random.fold_in(own_key, axis), (), 0, length) for axis, length in enumerate(entries.shape)]
    longest = entries.shape.index(max(entries.shape))
    neighbour = place[:longest] + [(place[longest] + 1) % entries.shape[longest]] + place[longest + 1:]
    return entries.at[tuple(place)].set(least).at[tuple(neighbour)].set(largest)


def steps_of(own_key, shape, pieces, low, largest):
    level, own = 1.0, jax.random.fold_in(own_key, 6)
    for axis_at, shards_of in pieces:
        steps = jnp.exp(jax.random.uniform(jax.random.fold_in(own, axis_at), (shards_of,), jnp.float32, low / len(pieces), largest / len(pieces)))
        level = level * jnp.repeat(steps, shape[axis_at] // shards_of).reshape([-1 if axis == axis_at else 1 for axis in range(len(shape))])
    return level


def scatter_about(key, extent, scale, limit, split=(), held_as=jnp.bfloat16):
    values = jax.random.normal(key, extent, jnp.float32) * scale
    if len(split) > 0:
        values = steps_of(key, extent, split, -0.22, 0.18) * values
    return jnp.clip(values, min=-limit, max=limit).astype(held_as)


def setup_inputs(seed: int = 0) -> dict:
    arg_keys = jax.random.split(jax.random.key(seed), 5)
    front = scatter_about(arg_keys[0], (FRONT, FRONT), (FRONT // 4) ** -0.5, 0.125, ((0, 8), (1, 4)))
    tile_mask = place_ends((jax.random.randint(arg_keys[1], (LEAVES, LEAVES), 0, 4) < 1).astype(jnp.int32), jax.random.fold_in(arg_keys[1], 1), 0, 1)
    probes = scatter_about(arg_keys[2], (FRONT, PROBES), 1.0, 6.0, ((0, 32),))
    coupling = scatter_about(arg_keys[3], (LEAVES * PROBES, PROBES), PROBES ** -0.5, 0.375, ((0, 32),), jnp.float32)
    return dict(front=front, tile_mask=tile_mask, probes=probes, coupling=coupling)


def matmul_high(left, right):
    return jnp.matmul(left, right, precision=lax.Precision.HIGHEST)

def transpose_last(array):
    return jnp.swapaxes(array, -1, -2)

def merge_pair(top_node, bottom_node, level_index):
    top_s, top_w, top_p = top_node
    bottom_s, bottom_w, bottom_p = bottom_node
    if level_index > 1:
        factor = 2.0 ** (-(level_index - 1) / 2.0)
        top_s = top_s - factor * matmul_high(top_p, bottom_w)
        bottom_s = bottom_s - factor * matmul_high(bottom_p, top_w)
    stacked = jnp.concatenate([top_s, bottom_s], axis=-2)
    gram_matrix = matmul_high(transpose_last(stacked), stacked)
    probe_count = gram_matrix.shape[-1]
    shift_value = 0.001 * (jnp.trace(gram_matrix, axis1=-2, axis2=-1) / probe_count + 1e-06)
    gram_matrix = gram_matrix + shift_value[..., None, None] * jnp.eye(probe_count, dtype=jnp.float32)
    lower_factor = jnp.linalg.cholesky(gram_matrix)
    basis_rows = jax.scipy.linalg.solve_triangular(lower_factor, transpose_last(stacked), lower=True)
    new_w = matmul_high(basis_rows, jnp.concatenate([top_w, bottom_w], axis=-2))
    row_total = top_s.shape[-2]
    top_half = transpose_last(basis_rows[..., :row_total])
    bottom_half = transpose_last(basis_rows[..., row_total:])
    return ((transpose_last(lower_factor), new_w, top_p + bottom_p), top_half, bottom_half)

def reference(front, tile_mask, probes, coupling):
    tile_rows = jnp.arange(LEAVES, dtype=jnp.int32)
    pair_keep = (tile_rows[:, None] // 2 != tile_rows[None, :] // 2).astype(jnp.float32)
    keep_tiles = tile_mask.astype(jnp.float32) * pair_keep
    probe_full = probes.astype(jnp.float32)

    def row_block(tile_index):
        rows = lax.dynamic_slice_in_dim(front, tile_index * LEAF, LEAF, 0).astype(jnp.float32)
        weights = lax.dynamic_index_in_dim(keep_tiles, tile_index, 0, keepdims=False)
        rows = (rows.reshape(LEAF, LEAVES, LEAF) * weights[None, :, None]).reshape(LEAF, FRONT)
        return jnp.dot(rows, probe_full, precision=lax.Precision.HIGHEST)
    samples = lax.map(row_block, jnp.arange(LEAVES, dtype=jnp.int32))
    node_state = (samples, probe_full.reshape(LEAVES, LEAF, PROBES), coupling.reshape(LEAVES, PROBES, PROBES))
    leaf_basis = None
    uppers = []
    for level_index in range(1, LEVELS + 1):
        node_count = node_state[0].shape[0]
        paired = tuple((array.reshape((node_count // 2, 2) + array.shape[1:]) for array in node_state))
        node_state, top_half, bottom_half = merge_pair(tuple((array[:, 0] for array in paired)), tuple((array[:, 1] for array in paired)), level_index)
        children = jnp.stack([top_half, bottom_half], axis=1).reshape((node_count,) + top_half.shape[1:])
        if level_index == 1:
            leaf_basis = children.reshape(FRONT, PROBES)
        else:
            spread = jnp.repeat(children, 2 ** (level_index - 1), axis=0)
            uppers.append(spread.reshape(LEAVES * PROBES, PROBES))
    return (leaf_basis, jnp.stack(uppers, axis=0))
```

```python
import functools

import jax
import jax.numpy as jnp
from jax import lax
from jax.experimental import pallas as pl
from jax.experimental.pallas import tpu as pltpu
from jax.sharding import PartitionSpec as P

F32 = jnp.float32
BF16 = jnp.bfloat16
SUB, LANE = 8, 128
PANEL = 2


def split(x):
    high = x.astype(BF16)
    return high, (x - high.astype(F32)).astype(BF16)


def product(left, right, dims):
    total = None
    for i in reversed(range(len(left))):
        for j in reversed(range(len(right))):
            if i + j >= 2:
                continue
            term = lax.dot_general(
                left[i], right[j], (((dims[0],), (dims[1],)), ((), ())), preferred_element_type=F32
            )
            total = term if total is None else total + term
    return total


def lane_copy(x, lane):
    return jnp.take_along_axis(
        x, jnp.full(x.shape, lane, jnp.int32), axis=1, mode="promise_in_bounds"
    )


def row_copy(x, row):
    return jnp.broadcast_to(x[row : row + 1, :], x.shape)


def tree_sum(terms):
    while len(terms) > 1:
        pairs = [terms[i] + terms[i + 1] for i in range(0, len(terms) - 1, 2)]
        terms = pairs + terms[len(pairs) * 2 :]
    return terms[0]


def factor_block(block, panel):
    count = LANE // SUB
    rows = [block[SUB * k : SUB * (k + 1), :] for k in range(count)]
    sub = lax.broadcasted_iota(jnp.int32, (SUB, LANE), 0)
    lane = lax.broadcasted_iota(jnp.int32, (SUB, LANE), 1)
    hot = [jnp.where(sub == s, 1.0, 0.0).astype(F32) for s in range(SUB)]
    inverse = [jnp.where(lane == sub + SUB * k, 1.0, 0.0).astype(F32) for k in range(count)]
    upper_out, inverse_out = [], []
    for first in range(0, count, panel):
        width, start = SUB * panel, SUB * first
        left, right = rows[first : first + panel], inverse[first : first + panel]
        cols = [[lane_copy(left[q], start + t) for q in range(panel)] for t in range(width)]
        done_left, done_right = [None] * panel, [None] * panel
        for s in range(width):
            own, at = divmod(s, SUB)
            pivot = row_copy(cols[s][own], at)
            scale = 1.0 / pivot
            root = lax.rsqrt(pivot)
            bare = [cols[s][q] - hot[at] if q == own else cols[s][q] for q in range(panel)]
            factor = [bare[q] * scale for q in range(panel)]
            left_row, right_row = row_copy(left[own], at), row_copy(right[own], at)
            if at == 0:
                done_left[own], done_right[own] = left_row * root, right_row * root
            else:
                here = sub == at
                done_left[own] = jnp.where(here, left_row * root, done_left[own])
                done_right[own] = jnp.where(here, right_row * root, done_right[own])
            for t in range(s + 1, width):
                across = row_copy(cols[t][own], at)
                for q in range(panel):
                    if t == s + 1:
                        cols[t][q] = cols[t][q] - (bare[q] * across) * scale
                    else:
                        cols[t][q] = cols[t][q] - factor[q] * across
            for q in range(panel):
                left[q] = left[q] - factor[q] * left_row
                right[q] = right[q] - factor[q] * right_row
        for q in range(panel):
            row = sub + SUB * (first + q)
            upper_out.append(jnp.where(lane >= row, done_left[q], 0.0))
            inverse_out.append(done_right[q])
        if first + panel < count:
            left_rows = [row_copy(left[s // SUB], s % SUB) for s in range(width)]
            right_rows = [row_copy(right[s // SUB], s % SUB) for s in range(width)]
            for k in range(first + panel, count):
                weight = [lane_copy(rows[k], start + s) for s in range(width)]
                rows[k] = rows[k] - tree_sum([weight[s] * left_rows[s] for s in range(width)])
                inverse[k] = inverse[k] - tree_sum(
                    [weight[s] * right_rows[s] for s in range(width)]
                )
    return jnp.concatenate(upper_out, axis=0), jnp.concatenate(inverse_out, axis=0)


def merge_math(own, other, level, outs):
    q_out, s_out, w_out = outs
    own_s, own_w, own_p = own
    other_s, other_w, other_p = other
    if level > 1:
        factor = 2.0 ** (-(level - 1) / 2.0)
        own_s = own_s - factor * product(own_p, other_w, (1, 0))
        other_s = other_s - factor * product(other_p, own_w, (1, 0))
    size = own_s.shape[1]
    half = size // 2
    own_h, other_h = split(own_s), split(other_s)
    gram = product(own_h, own_h, (0, 0)) + product(other_h, other_h, (0, 0))
    trace = jnp.sum(own_s * own_s) + jnp.sum(other_s * other_s)
    shift = 0.001 * (trace / size + 1e-06)
    eye = lax.broadcasted_iota(jnp.int32, (half, half), 0) == lax.broadcasted_iota(
        jnp.int32, (half, half), 1
    )
    diagonal = jnp.where(eye, shift, 0.0)
    upper_a, inverse_a = factor_block(gram[:half, :half] + diagonal, PANEL)
    inverse_a = split(inverse_a)
    upper_b = product(inverse_a, split(gram[:half, half:]), (1, 0))
    upper_b_parts = split(upper_b)
    rest = gram[half:, half:] + diagonal - product(upper_b_parts, upper_b_parts, (0, 0))
    upper_c, inverse_c = factor_block(rest, PANEL)
    inverse_c = split(inverse_c)
    s_out[:half, :half] = upper_a
    s_out[:half, half:] = upper_b
    s_out[half:, :half] = jnp.zeros((half, half), F32)
    s_out[half:, half:] = upper_c
    mixed = product(own_h, own_w, (0, 0)) + product(other_h, other_w, (0, 0))
    new_top = product(inverse_a, split(mixed[:half]), (1, 0))
    below = mixed[half:] - product(upper_b_parts, split(new_top), (0, 0))
    w_out[:half, :] = new_top
    w_out[half:, :] = product(inverse_c, split(below), (1, 0))
    q_left = product(tuple(x[:, :half] for x in own_h), inverse_a, (1, 1))
    remain = own_s[:, half:] - product(split(q_left), upper_b_parts, (1, 0))
    q_out[:, :half] = q_left
    q_out[:, half:] = product(split(remain), inverse_c, (1, 1))


def first_kernel(own_s, other_s, own_w, other_w, q_out, s_out, w_out):
    merge_math(
        (own_s[...], (own_w[...],), None),
        (other_s[...], (other_w[...],), None),
        1,
        (q_out, s_out, w_out),
    )


def join(is_first, near, far):
    return jnp.concatenate(
        [jnp.where(is_first, near, far), jnp.where(is_first, far, near)], axis=0
    )


def upper_kernel(
    level, side, own_s, own_w, own_p, near_s, far_s, near_w, far_w, other_p, q_out, s_out, w_out
):
    is_first = side[0] == 0
    other_s = join(is_first, near_s[...], far_s[...])
    other_w = join(is_first, near_w[...], far_w[...])
    merge_math(
        (own_s[...], split(own_w[...]), split(own_p[...])),
        (other_s, split(other_w), split(other_p[...])),
        level,
        (q_out, s_out, w_out),
    )


VMEM = pl.BlockSpec(memory_space=pltpu.VMEM)
SMEM = pl.BlockSpec(memory_space=pltpu.SMEM)


def first_merge(own_s, other_s, own_w, other_w):
    rows, size = own_s.shape
    return pl.pallas_call(
        first_kernel,
        out_shape=[
            jax.ShapeDtypeStruct((rows, size), F32),
            jax.ShapeDtypeStruct((size, size), F32),
            jax.ShapeDtypeStruct((size, size), F32),
        ],
        in_specs=[VMEM] * 4,
        out_specs=[VMEM] * 3,
        name="first_merge",
    )(own_s, other_s, own_w, other_w)


def upper_merge(level, side, arrays):
    size = arrays[0].shape[1]
    return pl.pallas_call(
        functools.partial(upper_kernel, level),
        out_shape=[jax.ShapeDtypeStruct((size, size), F32)] * 3,
        in_specs=[SMEM] + [VMEM] * 8,
        out_specs=[VMEM] * 3,
        name=f"merge_{level}",
    )(side, *arrays)


def partial_kernel(leaf, steps, ids, place, mask, front, *refs):
    chunks, out = refs[:steps], refs[steps]
    slot = pl.program_id(0)
    tile_row = place[1] ^ slot
    total = None
    for j in range(steps):
        chunk = ids[j]
        row_tile = place[0] * pl.num_programs(0) + tile_row
        col_tile = place[1] * steps + chunk
        keep = (mask[tile_row, chunk] != 0) & (row_tile // 2 != col_tile // 2)
        weight = jnp.where(keep, 1.0, 0.0).astype(F32)
        term = weight * lax.dot_general(
            front[:, pl.ds(pl.multiple_of(chunk * leaf, leaf), leaf)],
            chunks[j][...],
            (((1,), (0,)), ((), ())),
            preferred_element_type=F32,
        )
        total = term if total is None else total + term
    out[0] = total


def partial_samples(front, tile_mask, ids, place, chunks):
    leaf, size = chunks[0].shape
    slots = front.shape[0] // leaf
    steps = len(chunks)
    grid_spec = pltpu.PrefetchScalarGridSpec(
        num_scalar_prefetch=3,
        grid=(slots,),
        in_specs=[
            pl.BlockSpec((leaf, front.shape[1]), lambda k, ids, place, mask: (place[1] ^ k, 0))
        ]
        + [pl.BlockSpec((leaf, size), lambda k, ids, place, mask: (0, 0))] * steps,
        out_specs=pl.BlockSpec((1, leaf, size), lambda k, ids, place, mask: (k, 0, 0)),
    )
    return pl.pallas_call(
        functools.partial(partial_kernel, leaf, steps),
        out_shape=jax.ShapeDtypeStruct((slots, leaf, size), F32),
        grid_spec=grid_spec,
        name="partial_samples",
    )(ids, place, tile_mask, front, *chunks)


def swap(x, axis, bit):
    return lax.ppermute(x, axis, [(i, i ^ (1 << bit)) for i in range(lax.axis_size(axis))])


def shift(x, axis, by):
    count = lax.axis_size(axis)
    return lax.ppermute(x, axis, [(i, (i + by) % count) for i in range(count)])


def shards(front, tile_mask, probes, coupling):
    col_count, row_count = lax.axis_size("col"), lax.axis_size("row")
    row_index, col_index = lax.axis_index("row"), lax.axis_index("col")
    col_levels, row_levels = col_count.bit_length() - 1, row_count.bit_length() - 1

    pairs = [
        ((b % row_count) * col_count + b // row_count, b) for b in range(row_count * col_count)
    ]
    own_w = lax.ppermute(probes, ("row", "col"), pairs)
    other_w = swap(own_w, "col", 0)

    chunks, held = [], probes
    for step in range(row_count // 2):
        chunks.append(held)
        chunks.append(swap(held, "row", 0))
        if step < row_count // 2 - 1:
            held = shift(held, "row", 2)
    ids = []
    for step in range(row_count // 2):
        from_row = (row_index - 2 * step) % row_count
        ids += [from_row, from_row ^ 1]
    ids = jnp.stack(ids).astype(jnp.int32)
    place = jnp.stack([row_index, col_index]).astype(jnp.int32)

    slots = partial_samples(front, tile_mask, ids, place, chunks)
    slots = [slots[k] for k in range(col_count)]
    for bit in range(col_levels):
        step = 1 << bit
        keep = list(range(0, col_count, 2 * step))
        got = swap(jnp.stack([slots[k + step] for k in keep]), "col", bit)
        for i, k in enumerate(keep):
            slots[k] = slots[k] + got[i]
    own_s = slots[0]

    other_p = swap(coupling, "col", 0)
    own_p = coupling + other_p

    halves = []
    other_s = swap(own_s, "col", 0)
    q, s, w = first_merge(own_s, other_s, own_w, other_w)
    halves.append(q)
    side = (col_index & 1).astype(jnp.int32)[None]
    half = s.shape[0] // 2
    bits = [("col", b) for b in range(1, col_levels)] + [("row", b) for b in range(row_levels)]
    for level, (axis, bit) in enumerate(bits, start=2):
        other_p = swap(own_p, axis, bit)
        near_w = swap(lax.dynamic_slice_in_dim(w, side[0] * half, half, 0), axis, bit)
        near_s = swap(lax.dynamic_slice_in_dim(s, side[0] * half, half, 0), axis, bit)
        far_w = swap(near_w, "col", 0)
        far_s = swap(near_s, "col", 0)
        q, s, w = upper_merge(
            level, side, (s, w, own_p, near_s, far_s, near_w, far_w, other_p)
        )
        own_p = own_p + other_p
        halves.append(q)
    return (halves[0], jnp.stack(halves[1:], axis=0))


def solution(mesh):
    in_specs = (P("row", "col"), P("row", "col"), P(("col", "row"), None), P(("row", "col"), None))
    out_specs = (P(("row", "col"), None), P(None, ("row", "col"), None))
    return jax.shard_map(shards, mesh=mesh, in_specs=in_specs, out_specs=out_specs, check_vma=False)
```

```python
import functools

import jax
import jax.numpy as jnp
from jax import lax
from jax.experimental import pallas as pl
from jax.experimental.pallas import tpu as pltpu
from jax.sharding import PartitionSpec as P

F32 = jnp.float32
BF16 = jnp.bfloat16
SUB, LANE = 8, 128
BLOCK = LANE // 2
PANEL = 2


def split(x):
    high = x.astype(BF16)
    return high, (x - high.astype(F32)).astype(BF16)


def dot(left, right, dims):
    return lax.dot_general(
        left, right, (((dims[0],), (dims[1],)), ((), ())), preferred_element_type=F32
    )


def product(left, right, dims):
    total = None
    for i in reversed(range(len(left))):
        for j in reversed(range(len(right))):
            if i + j < 2:
                term = dot(left[i], right[j], dims)
                total = term if total is None else total + term
    return total


def lane_copy(x, lane):
    return jnp.take_along_axis(
        x, jnp.full(x.shape, lane, jnp.int32), axis=1, mode="promise_in_bounds"
    )


def row_copy(x, row):
    return jnp.broadcast_to(x[row : row + 1, :], x.shape)


def tree_sum(terms):
    while len(terms) > 1:
        pairs = [terms[i] + terms[i + 1] for i in range(0, len(terms) - 1, 2)]
        terms = pairs + terms[len(pairs) * 2 :]
    return terms[0]


def factor_block(packed, offset):
    count = BLOCK // SUB
    rows = [packed[SUB * k : SUB * (k + 1), :] for k in range(count)]
    sub = lax.broadcasted_iota(jnp.int32, (SUB, LANE), 0)
    out = []
    for first in range(0, count, PANEL):
        width, start = SUB * PANEL, offset + SUB * first
        held = rows[first : first + PANEL]
        cols = [[lane_copy(held[q], start + t) for q in range(PANEL)] for t in range(width)]
        done, scales = [None] * PANEL, [None] * PANEL
        for s in range(width):
            own, at = divmod(s, SUB)
            if at == 0:
                for t in range(s, width):
                    for q in range(own):
                        cols[t][q] = lane_copy(held[q], start + t)
            here = sub == at
            pivot = row_copy(cols[s][own], at)
            scale = 1.0 / pivot
            root = lax.rsqrt(pivot)
            bare = [jnp.where(here, 0.0, cols[s][q]) if q == own else cols[s][q] for q in range(PANEL)]
            factor = [x * scale for x in bare]
            row = row_copy(held[own], at)
            if at == 0:
                done[own], scales[own] = row * root, scale
            else:
                done[own] = jnp.where(here, row * root, done[own])
                scales[own] = jnp.where(here, scale, scales[own])
            for t in range(s + 1, width):
                across = row_copy(cols[s][t // SUB], t % SUB)
                for q in range(PANEL):
                    if q < t // SUB and own < t // SUB:
                        continue
                    if t == s + 1:
                        cols[t][q] = cols[t][q] - (bare[q] * across) * scale
                    else:
                        cols[t][q] = cols[t][q] - factor[q] * across
            for q in range(PANEL):
                held[q] = held[q] - factor[q] * row
        out += done
        if first + PANEL < count:
            held = [held[q] * scales[q] for q in range(PANEL)]
            solved = [row_copy(held[s // SUB], s % SUB) for s in range(width)]
            for k in range(first + PANEL, count):
                weight = [lane_copy(rows[k], start + s) for s in range(width)]
                rows[k] = rows[k] - tree_sum([weight[s] * solved[s] for s in range(width)])
    return jnp.concatenate(out, axis=0)


def four(x):
    high, low = split(x)
    return jnp.concatenate([high, high, low, low], axis=0)


def two_parts(x):
    high = x.astype(BF16).astype(F32)
    return high, x - high


def factor_all(gram, rights):
    count = gram.shape[0] // BLOCK
    lane = lax.broadcasted_iota(jnp.int32, (BLOCK, LANE), 1)
    sub = lax.broadcasted_iota(jnp.int32, (BLOCK, LANE), 0)
    blocks = [gram[BLOCK * i : BLOCK * (i + 1), :] for i in range(count)]
    rights = [[x[BLOCK * i : BLOCK * (i + 1), :] for i in range(count)] for x in rights]
    upper, solved = [], [[] for _ in rights]
    for i in range(count):
        first, offset = BLOCK * i // LANE * LANE, BLOCK * i % LANE
        other = BLOCK - offset
        mine = (lane >= offset) & (lane < offset + BLOCK)
        tile = slice(first, first + LANE)
        both = factor_block(
            jnp.where(mine, blocks[i][:, tile], jnp.where(lane - other == sub, 1.0, 0.0)), offset
        )
        high, low = two_parts(jnp.where(mine, 0.0, both))
        low_here = pltpu.roll(low, BLOCK, 1)
        left = jnp.concatenate([jnp.where(mine, low_here, high), high], axis=1).astype(BF16)
        right = [dot(left, four(x[i]), (1, 0)) for x in rights]
        for x, y in zip(solved, right):
            x.append(y)
        row = both
        if i + 1 < count:
            high_here = pltpu.roll(high, BLOCK, 1)
            across = jnp.concatenate([high_here, low_here, high_here], axis=1).astype(BF16)
            below = jnp.concatenate([blocks[j][:, tile] for j in range(i + 1, count)], axis=0)
            high, low = split(below)
            column = dot(
                jnp.concatenate([high, high, low], axis=1),
                jnp.concatenate([across, across], axis=0),
                (1, 1),
            )
            row = dot(left, four(blocks[i][:, first:]), (1, 0))
            high, low = two_parts(column)
            near = lax.broadcasted_iota(jnp.int32, column.shape, 1) < BLOCK
            column = jnp.concatenate(
                [jnp.where(near, high, low), jnp.where(near, high, 0.0)], axis=1
            ).astype(BF16)
            change = dot(column, four(row), (1, 0))
            for j in range(i + 1, count):
                at = BLOCK * (j - i - 1)
                new = blocks[j][:, first:] - change[at : at + BLOCK, :]
                if first:
                    new = jnp.concatenate([blocks[j][:, :first], new], axis=1)
                blocks[j] = new
            for x, y in zip(rights, right):
                change = dot(column, four(y), (1, 0))
                for j in range(i + 1, count):
                    at = BLOCK * (j - i - 1)
                    x[j] = x[j] - change[at : at + BLOCK, :]
        head = jnp.where(mine, both, row[:, :LANE])
        head = jnp.where(lane < offset + jnp.where(mine, sub, 0), 0.0, head)
        upper.append(head if row.shape[1] == LANE else jnp.concatenate([head, row[:, LANE:]], axis=1))
    return upper, [jnp.concatenate(x, axis=0) for x in solved]


def merge_math(own, other, level, want_state):
    own_s, own_w, own_p = own
    other_s, other_w, other_p = other
    if level > 1:
        factor = 2.0 ** (-(level - 1) / 2.0)
        own_s = own_s - factor * product(own_p, other_w, (1, 0))
        other_s = other_s - factor * product(other_p, own_w, (1, 0))
    size = own_s.shape[1]
    own_h, other_h = split(own_s), split(other_s)
    gram = product(own_h, own_h, (0, 0)) + product(other_h, other_h, (0, 0))
    trace = jnp.sum(own_s * own_s) + jnp.sum(other_s * other_s)
    shift = 0.001 * (trace / size + 1e-06)
    eye = lax.broadcasted_iota(jnp.int32, (size, size), 0) == lax.broadcasted_iota(
        jnp.int32, (size, size), 1
    )
    rights = [jnp.where(eye, 1.0, 0.0)]
    if want_state:
        rights.append(product(own_h, own_w, (0, 0)) + product(other_h, other_w, (0, 0)))
    upper, solved = factor_all(gram + jnp.where(eye, shift, 0.0), rights)
    q = product(own_h, split(solved[0]), (1, 1))
    return q, upper, solved[1] if want_state else None


def store_state(side, upper, w, state, send):
    half = w.shape[0] // 2
    part = half // 2
    share = half - part // 2
    state[0, :half] = w[:half]
    state[1, :half] = w[half:]
    top = jnp.concatenate(upper[:2], axis=0)
    state[0, half:] = top[:share]
    state[1, half : half + half - share] = top[share:]
    state[1, half + half - share :] = jnp.concatenate(upper[2:], axis=1)
    send[...] = state[side[0]]


def load_state(first, second):
    half = first.shape[1] // 2
    part = half // 2
    share = half - part // 2
    w = jnp.concatenate([first[:half], second[:half]], axis=0)
    split_at = half + half - share
    top = jnp.concatenate([first[half:], second[half:split_at]], axis=0)
    last = second[split_at:]
    corner = jnp.concatenate([last[:, :half], last[:, half:]], axis=0)
    bottom = jnp.concatenate([jnp.zeros((half, half), F32), corner], axis=1)
    return jnp.concatenate([top, bottom], axis=0), w


def first_kernel(
    side, own_a, own_b, other_a, other_b, own_w, other_w, q_out, state, send
):
    q, upper, w = merge_math(
        (own_a[...] + own_b[...], (own_w[...],), None),
        (other_a[...] + other_b[...], (other_w[...],), None),
        1,
        True,
    )
    store_state(side, upper, w, state, send)
    q_out[...] = q


def upper_kernel(level, is_last, has_buffer, side, own, own_p, near, far, other_p, *refs):
    refs = list(refs)
    if has_buffer:
        refs.pop(0)
    q_all = refs.pop(0)
    outs = [] if is_last else [refs.pop(0), refs.pop(0)]
    q_here, done = refs
    is_first = side[0] == 0
    own_s, own_w = load_state(own[0], own[1])
    near, far = near[...], far[...]
    other_s, other_w = load_state(jnp.where(is_first, near, far), jnp.where(is_first, far, near))
    q, upper, w = merge_math(
        (own_s, split(own_w), split(own_p[...])),
        (other_s, split(other_w), split(other_p[...])),
        level,
        not is_last,
    )
    q_here[...] = q
    copy = pltpu.make_async_copy(q_here, q_all.at[level - 2], done)
    copy.start()
    if not is_last:
        store_state(side, upper, w, *outs)
    copy.wait()


VMEM = pl.BlockSpec(memory_space=pltpu.VMEM)
SMEM = pl.BlockSpec(memory_space=pltpu.SMEM)
ANY = pl.BlockSpec(memory_space=pl.ANY)


def state_shapes(size):
    rows = size // 2 + 3 * size // 8
    return [
        jax.ShapeDtypeStruct((2, rows, size), F32),
        jax.ShapeDtypeStruct((rows, size), F32),
    ]


def first_merge(side, arrays):
    rows, size = arrays[0].shape
    return pl.pallas_call(
        first_kernel,
        out_shape=[jax.ShapeDtypeStruct((rows, size), F32)] + state_shapes(size),
        in_specs=[SMEM] + [VMEM] * len(arrays),
        out_specs=[VMEM] * 3,
        name="first_merge",
    )(side, *arrays)


def upper_merge(level, levels, side, arrays, buffer):
    size = arrays[1].shape[1]
    is_last = level == levels
    extra = [] if buffer is None else [buffer]
    out_shape = [jax.ShapeDtypeStruct((levels - 1, size, size), F32)]
    out_shape += [] if is_last else state_shapes(size)
    return pl.pallas_call(
        functools.partial(upper_kernel, level, is_last, bool(extra)),
        out_shape=out_shape,
        in_specs=[SMEM] + [VMEM] * len(arrays) + [ANY] * len(extra),
        out_specs=[ANY] + [VMEM] * (len(out_shape) - 1),
        scratch_shapes=[pltpu.VMEM((size, size), F32), pltpu.SemaphoreType.DMA(())],
        input_output_aliases={1 + len(arrays): 0} if extra else {},
        name=f"merge_{level}",
    )(side, *arrays, *extra)


def sample_kernel(row_tiles, keys, start, place, mask, *refs):
    count = len(keys)
    tiles, chunks = refs[:count], refs[count : 2 * count]
    total = None if not start else refs[2 * count][0]
    outs = refs[2 * count + start :]
    slot = pl.program_id(0)
    tile_row = place[1] ^ slot
    for j, key in enumerate(keys):
        chunk = place[0] ^ key
        row_tile = place[0] * pl.num_programs(0) + tile_row
        col_tile = place[1] * row_tiles + chunk
        keep = (mask[tile_row, chunk] != 0) & (row_tile // 2 != col_tile // 2)
        term = dot(tiles[j][...], chunks[j][...], (1, 0))
        term = jnp.where(keep, term, 0.0)
        total = term if total is None else total + term
    if len(outs) == 1:
        outs[0][0] = total
    else:

        @pl.when(slot % 2 == 0)
        def _():
            outs[0][0] = total

        @pl.when(slot % 2 == 1)
        def _():
            outs[1][0] = total


def add_samples(front, tile_mask, place, chunks, keys, start, last):
    leaf, size = chunks[0].shape
    slots, row_tiles = front.shape[0] // leaf, front.shape[1] // leaf

    def tile_of(key):
        return lambda k, place, mask: (place[1] ^ k, place[0] ^ key)

    block = lambda k, place, mask: (k, 0, 0)
    pair = lambda k, place, mask: (k // 2, 0, 0)
    extra = [] if start is None else [start]
    if last:
        out_shape = [jax.ShapeDtypeStruct((slots // 2, leaf, size), F32)] * 2
        out_specs = [pl.BlockSpec((1, leaf, size), pair)] * 2
    else:
        out_shape = [jax.ShapeDtypeStruct((slots, leaf, size), F32)]
        out_specs = [pl.BlockSpec((1, leaf, size), block)]
    grid_spec = pltpu.PrefetchScalarGridSpec(
        num_scalar_prefetch=2,
        grid=(slots,),
        in_specs=[pl.BlockSpec((leaf, leaf), tile_of(key)) for key in keys]
        + [pl.BlockSpec((leaf, size), lambda k, place, mask: (0, 0))] * len(keys)
        + [pl.BlockSpec((1, leaf, size), block)] * len(extra),
        out_specs=out_specs,
    )
    return pl.pallas_call(
        functools.partial(sample_kernel, row_tiles, keys, len(extra)),
        out_shape=out_shape,
        grid_spec=grid_spec,
        name="last_samples" if last else "samples",
    )(place, tile_mask, *[front] * len(keys), *chunks, *extra)


def swap(x, axis, bit):
    return lax.ppermute(x, axis, [(i, i ^ (1 << bit)) for i in range(lax.axis_size(axis))])


def shards(front, tile_mask, probes, coupling):
    col_count, row_count = lax.axis_size("col"), lax.axis_size("row")
    row_index, col_index = lax.axis_index("row"), lax.axis_index("col")
    col_levels, row_levels = col_count.bit_length() - 1, row_count.bit_length() - 1
    levels = col_levels + row_levels
    place = jnp.stack([row_index, col_index]).astype(jnp.int32)
    side = (col_index & 1).astype(jnp.int32)[None]

    chunks = {0: probes}
    chunks[1] = swap(probes, "row", 0)
    for bit in range(row_levels - 1, 0, -1):
        for key in list(chunks):
            new = key | 1 << bit
            if key == 1:
                chunks[new] = swap(chunks[new ^ 1], "row", 0)
            else:
                chunks[new] = swap(chunks[key], "row", bit)

    pairs = [
        ((b % row_count) * col_count + b // row_count, b) for b in range(row_count * col_count)
    ]
    own_w = lax.ppermute(probes, ("row", "col"), pairs)
    other_w = swap(own_w, "col", 0)
    other_p = swap(coupling, "col", 0)
    own_p = coupling + other_p

    order = list(chunks)
    early, late = order[:-2], order[-2:]
    (part,) = add_samples(front, tile_mask, place, [chunks[k] for k in early], early, None, False)
    keep, send = add_samples(front, tile_mask, place, [chunks[k] for k in late], late, part, True)
    got = swap(send, "col", 0)
    slots = {2 * k: (keep[k], got[k]) for k in range(col_count // 2)}
    for bit in range(1, col_levels):
        step = 1 << bit
        left = list(range(0, col_count, 2 * step))
        moved = swap(jnp.stack([slots[k + step][0] + slots[k + step][1] for k in left]), "col", bit)
        slots = {k: (slots[k][0] + slots[k][1], moved[i]) for i, k in enumerate(left)}
    own_a, own_b = slots[0]
    other_a, other_b = swap(own_a, "col", 0), swap(own_b, "col", 0)

    leaf_basis, state, send = first_merge(
        side, (own_a, own_b, other_a, other_b, own_w, other_w)
    )
    buffer = None
    bits = [("col", b) for b in range(1, col_levels)] + [("row", b) for b in range(row_levels)]
    for level, (axis, bit) in enumerate(bits, start=2):
        other_p = swap(own_p, axis, bit)
        near = swap(send, axis, bit)
        far = swap(near, "col", 0)
        buffer, *rest = upper_merge(
            level, levels, side, (state, own_p, near, far, other_p), buffer
        )
        own_p = own_p + other_p
        if rest:
            state, send = rest
    return (leaf_basis, buffer)


def solution(mesh):
    in_specs = (P("row", "col"), P("row", "col"), P(("col", "row"), None), P(("row", "col"), None))
    out_specs = (P(("row", "col"), None), P(None, ("row", "col"), None))
    return jax.shard_map(shards, mesh=mesh, in_specs=in_specs, out_specs=out_specs, check_vma=False)
```

```python
import functools

import jax
import jax.numpy as jnp
from jax import lax
from jax.experimental import pallas as pl
from jax.experimental.pallas import tpu as pltpu
from jax.sharding import PartitionSpec as P

F32 = jnp.float32
BF16 = jnp.bfloat16
SUB, LANE = 8, 128
BLOCK = LANE // 2
PANEL = 2


def split(x):
    high = x.astype(BF16)
    return high, (x - high.astype(F32)).astype(BF16)


def dot(left, right, dims):
    return lax.dot_general(
        left, right, (((dims[0],), (dims[1],)), ((), ())), preferred_element_type=F32
    )


def product(left, right, dims):
    total = None
    for i in reversed(range(len(left))):
        for j in reversed(range(len(right))):
            if i + j < 2:
                term = dot(left[i], right[j], dims)
                total = term if total is None else total + term
    return total


def lane_copy(x, lane):
    return jnp.take_along_axis(
        x, jnp.full(x.shape, lane, jnp.int32), axis=1, mode="promise_in_bounds"
    )


def row_copy(x, row):
    return jnp.broadcast_to(x[row : row + 1, :], x.shape)


def tree_sum(terms):
    while len(terms) > 1:
        pairs = [terms[i] + terms[i + 1] for i in range(0, len(terms) - 1, 2)]
        terms = pairs + terms[len(pairs) * 2 :]
    return terms[0]


def factor_block(packed, offset):
    count = BLOCK // SUB
    rows = [packed[SUB * k : SUB * (k + 1), :] for k in range(count)]
    sub = lax.broadcasted_iota(jnp.int32, (SUB, LANE), 0)
    out = []
    for first in range(0, count, PANEL):
        width, start = SUB * PANEL, offset + SUB * first
        held = rows[first : first + PANEL]
        cols = [[lane_copy(held[q], start + t) for q in range(PANEL)] for t in range(width)]
        done, scales = [None] * PANEL, [None] * PANEL
        for s in range(width):
            own, at = divmod(s, SUB)
            if at == 0:
                for t in range(s, width):
                    for q in range(own):
                        cols[t][q] = lane_copy(held[q], start + t)
            here = sub == at
            pivot = row_copy(cols[s][own], at)
            scale = 1.0 / pivot
            root = lax.rsqrt(pivot)
            bare = [jnp.where(here, 0.0, cols[s][q]) if q == own else cols[s][q] for q in range(PANEL)]
            factor = [x * scale for x in bare]
            row = row_copy(held[own], at)
            if at == 0:
                done[own], scales[own] = row * root, scale
            else:
                done[own] = jnp.where(here, row * root, done[own])
                scales[own] = jnp.where(here, scale, scales[own])
            for t in range(s + 1, width):
                across = row_copy(cols[s][t // SUB], t % SUB)
                for q in range(PANEL):
                    if q < t // SUB and own < t // SUB:
                        continue
                    if t == s + 1:
                        cols[t][q] = cols[t][q] - (bare[q] * across) * scale
                    else:
                        cols[t][q] = cols[t][q] - factor[q] * across
            for q in range(PANEL):
                held[q] = held[q] - factor[q] * row
        out += done
        if first + PANEL < count:
            held = [held[q] * scales[q] for q in range(PANEL)]
            solved = [row_copy(held[s // SUB], s % SUB) for s in range(width)]
            for k in range(first + PANEL, count):
                weight = [lane_copy(rows[k], start + s) for s in range(width)]
                rows[k] = rows[k] - tree_sum([weight[s] * solved[s] for s in range(width)])
    return jnp.concatenate(out, axis=0)


def four(x):
    high, low = split(x)
    return jnp.concatenate([high, high, low, low], axis=0)


def two_parts(x):
    high = x.astype(BF16).astype(F32)
    return high, x - high


def factor_all(gram, rights):
    count = gram.shape[0] // BLOCK
    lane = lax.broadcasted_iota(jnp.int32, (BLOCK, LANE), 1)
    sub = lax.broadcasted_iota(jnp.int32, (BLOCK, LANE), 0)
    blocks = [gram[BLOCK * i : BLOCK * (i + 1), :] for i in range(count)]
    rights = [[x[BLOCK * i : BLOCK * (i + 1), :] for i in range(count)] for x in rights]
    upper, solved = [], [[] for _ in rights]
    for i in range(count):
        first, offset = BLOCK * i // LANE * LANE, BLOCK * i % LANE
        other = BLOCK - offset
        mine = (lane >= offset) & (lane < offset + BLOCK)
        tile = slice(first, first + LANE)
        both = factor_block(
            jnp.where(mine, blocks[i][:, tile], jnp.where(lane - other == sub, 1.0, 0.0)), offset
        )
        high, low = two_parts(jnp.where(mine, 0.0, both))
        low_here = pltpu.roll(low, BLOCK, 1)
        left = jnp.concatenate([jnp.where(mine, low_here, high), high], axis=1).astype(BF16)
        right = [dot(left, four(x[i]), (1, 0)) for x in rights]
        for x, y in zip(solved, right):
            x.append(y)
        row = both
        if i + 1 < count:
            high_here = pltpu.roll(high, BLOCK, 1)
            across = jnp.concatenate([high_here, low_here, high_here], axis=1).astype(BF16)
            below = jnp.concatenate([blocks[j][:, tile] for j in range(i + 1, count)], axis=0)
            high, low = split(below)
            column = dot(
                jnp.concatenate([high, high, low], axis=1),
                jnp.concatenate([across, across], axis=0),
                (1, 1),
            )
            row = dot(left, four(blocks[i][:, first:]), (1, 0))
            high, low = two_parts(column)
            near = lax.broadcasted_iota(jnp.int32, column.shape, 1) < BLOCK
            column = jnp.concatenate(
                [jnp.where(near, high, low), jnp.where(near, high, 0.0)], axis=1
            ).astype(BF16)
            change = dot(column, four(row), (1, 0))
            for j in range(i + 1, count):
                at = BLOCK * (j - i - 1)
                new = blocks[j][:, first:] - change[at : at + BLOCK, :]
                if first:
                    new = jnp.concatenate([blocks[j][:, :first], new], axis=1)
                blocks[j] = new
            for x, y in zip(rights, right):
                change = dot(column, four(y), (1, 0))
                for j in range(i + 1, count):
                    at = BLOCK * (j - i - 1)
                    x[j] = x[j] - change[at : at + BLOCK, :]
        head = jnp.where(mine, both, row[:, :LANE])
        head = jnp.where(lane < offset + jnp.where(mine, sub, 0), 0.0, head)
        upper.append(head if row.shape[1] == LANE else jnp.concatenate([head, row[:, LANE:]], axis=1))
    return upper, [jnp.concatenate(x, axis=0) for x in solved]


def merge_math(own, other, level, want_state):
    own_s, own_w, own_p = own
    other_s, other_w, other_p = other
    if level > 1:
        factor = 2.0 ** (-(level - 1) / 2.0)
        own_s = own_s - factor * product(own_p, other_w, (1, 0))
        other_s = other_s - factor * product(other_p, own_w, (1, 0))
    size = own_s.shape[1]
    own_h, other_h = split(own_s), split(other_s)
    gram = product(own_h, own_h, (0, 0)) + product(other_h, other_h, (0, 0))
    trace = jnp.sum(own_s * own_s) + jnp.sum(other_s * other_s)
    shift = 0.001 * (trace / size + 1e-06)
    eye = lax.broadcasted_iota(jnp.int32, (size, size), 0) == lax.broadcasted_iota(
        jnp.int32, (size, size), 1
    )
    rights = [jnp.where(eye, 1.0, 0.0)]
    if want_state:
        rights.append(product(own_h, own_w, (0, 0)) + product(other_h, other_w, (0, 0)))
    upper, solved = factor_all(gram + jnp.where(eye, shift, 0.0), rights)
    q = product(own_h, split(solved[0]), (1, 1))
    return q, upper, solved[1] if want_state else None


def store_state(side, upper, w, state, send):
    half = w.shape[0] // 2
    part = half // 2
    share = half - part // 2
    state[0, :half] = w[:half]
    state[1, :half] = w[half:]
    top = jnp.concatenate(upper[:2], axis=0)
    state[0, half:] = top[:share]
    state[1, half : half + half - share] = top[share:]
    state[1, half + half - share :] = jnp.concatenate(upper[2:], axis=1)
    send[...] = state[side[0]]


def load_state(first, second):
    half = first.shape[1] // 2
    part = half // 2
    share = half - part // 2
    w = jnp.concatenate([first[:half], second[:half]], axis=0)
    split_at = half + half - share
    top = jnp.concatenate([first[half:], second[half:split_at]], axis=0)
    last = second[split_at:]
    corner = jnp.concatenate([last[:, :half], last[:, half:]], axis=0)
    bottom = jnp.concatenate([jnp.zeros((half, half), F32), corner], axis=1)
    return jnp.concatenate([top, bottom], axis=0), w


def first_kernel(
    side, own_a, own_b, other_a, other_b, own_w, other_w, q_out, state, send
):
    q, upper, w = merge_math(
        (own_a[...] + own_b[...], (own_w[...],), None),
        (other_a[...] + other_b[...], (other_w[...],), None),
        1,
        True,
    )
    store_state(side, upper, w, state, send)
    q_out[...] = q


def upper_kernel(level, is_last, has_buffer, side, own, own_p, near, far, other_p, *refs):
    refs = list(refs)
    if has_buffer:
        refs.pop(0)
    q_all = refs.pop(0)
    outs = [] if is_last else [refs.pop(0), refs.pop(0)]
    q_here, done = refs
    is_first = side[0] == 0
    own_s, own_w = load_state(own[0], own[1])
    near, far = near[...], far[...]
    other_s, other_w = load_state(jnp.where(is_first, near, far), jnp.where(is_first, far, near))
    q, upper, w = merge_math(
        (own_s, split(own_w), split(own_p[...])),
        (other_s, split(other_w), split(other_p[...])),
        level,
        not is_last,
    )
    q_here[...] = q
    copy = pltpu.make_async_copy(q_here, q_all.at[level - 2], done)
    copy.start()
    if not is_last:
        store_state(side, upper, w, *outs)
    copy.wait()


VMEM = pl.BlockSpec(memory_space=pltpu.VMEM)
SMEM = pl.BlockSpec(memory_space=pltpu.SMEM)
ANY = pl.BlockSpec(memory_space=pl.ANY)


def state_shapes(size):
    rows = size // 2 + 3 * size // 8
    return [
        jax.ShapeDtypeStruct((2, rows, size), F32),
        jax.ShapeDtypeStruct((rows, size), F32),
    ]


def first_merge(side, arrays):
    rows, size = arrays[0].shape
    return pl.pallas_call(
        first_kernel,
        out_shape=[jax.ShapeDtypeStruct((rows, size), F32)] + state_shapes(size),
        in_specs=[SMEM] + [VMEM] * len(arrays),
        out_specs=[VMEM] * 3,
        name="first_merge",
    )(side, *arrays)


def upper_merge(level, levels, side, arrays, buffer):
    size = arrays[1].shape[1]
    is_last = level == levels
    extra = [] if buffer is None else [buffer]
    out_shape = [jax.ShapeDtypeStruct((levels - 1, size, size), F32)]
    out_shape += [] if is_last else state_shapes(size)
    return pl.pallas_call(
        functools.partial(upper_kernel, level, is_last, bool(extra)),
        out_shape=out_shape,
        in_specs=[SMEM] + [VMEM] * len(arrays) + [ANY] * len(extra),
        out_specs=[ANY] + [VMEM] * (len(out_shape) - 1),
        scratch_shapes=[pltpu.VMEM((size, size), F32), pltpu.SemaphoreType.DMA(())],
        input_output_aliases={1 + len(arrays): 0} if extra else {},
    )(side, *arrays, *extra)


def sample_kernel(keys, place, mask, front, *refs):
    count = len(keys)
    chunks, (keep, send, tiles, arrived) = refs[:count], refs[count:]
    leaf = chunks[0].shape[0]
    slots = 2 * keep.shape[0]
    order = [*range(1, slots, 2), *range(0, slots, 2)]
    present, copies = {}, {}
    for slot in order:
        tile_row = place[1] ^ slot
        for j, key in enumerate(keys):
            chunk = place[0] ^ key
            row_tile = place[0] * slots + tile_row
            col_tile = place[1] * count + chunk
            present[slot, j] = (mask[tile_row, chunk] != 0) & (row_tile // 2 != col_tile // 2)
            copies[slot, j] = pltpu.make_async_copy(
                front.at[
                    pl.ds(pl.multiple_of(tile_row * leaf, leaf), leaf),
                    pl.ds(pl.multiple_of(chunk * leaf, leaf), leaf),
                ],
                tiles.at[slot, j],
                arrived.at[slot, j],
            )

            @pl.when(present[slot, j])
            def _():
                copies[slot, j].start()

    for slot in order:
        for j in range(count):

            @pl.when(present[slot, j])
            def _():
                copies[slot, j].wait()

        total = None
        for j in range(count):
            tile = jnp.where(present[slot, j], tiles[slot, j], jnp.zeros((), BF16))
            term = dot(tile, chunks[j][...], (1, 0))
            total = term if total is None else total + term
        out = send if slot % 2 else keep
        out[slot // 2] = total


def all_samples(front, tile_mask, place, chunks, keys):
    leaf, size = chunks[0].shape
    slots = front.shape[0] // leaf
    return pl.pallas_call(
        functools.partial(sample_kernel, keys),
        out_shape=[jax.ShapeDtypeStruct((slots // 2, leaf, size), F32)] * 2,
        in_specs=[SMEM, SMEM, ANY] + [VMEM] * len(keys),
        out_specs=[VMEM] * 2,
        scratch_shapes=[
            pltpu.VMEM((slots, len(keys), leaf, leaf), BF16),
            pltpu.SemaphoreType.DMA((slots, len(keys))),
        ],
        name="samples",
    )(place, tile_mask, front, *chunks)


def swap(x, axis, bit):
    return lax.ppermute(x, axis, [(i, i ^ (1 << bit)) for i in range(lax.axis_size(axis))])


def step(front, tile_mask, probes, coupling):
    col_count, row_count = lax.axis_size("col"), lax.axis_size("row")
    row_index, col_index = lax.axis_index("row"), lax.axis_index("col")
    col_levels, row_levels = col_count.bit_length() - 1, row_count.bit_length() - 1
    levels = col_levels + row_levels
    place = jnp.stack([row_index, col_index]).astype(jnp.int32)
    side = (col_index & 1).astype(jnp.int32)[None]
    bits = [("col", b) for b in range(col_levels)] + [("row", b) for b in range(row_levels)]

    chunks = {0: probes}
    chunks[1] = swap(probes, "row", 0)
    for bit in range(row_levels - 1, 0, -1):
        for key in list(chunks):
            new = key | 1 << bit
            if key == 1:
                chunks[new] = swap(chunks[new ^ 1], "row", 0)
            else:
                chunks[new] = swap(chunks[key], "row", bit)

    pairs = [
        ((b % row_count) * col_count + b // row_count, b) for b in range(row_count * col_count)
    ]
    own_w = lax.ppermute(probes, ("row", "col"), pairs)
    other_w = swap(own_w, "col", 0)

    own_p, other_p, total_p = {}, {}, coupling
    for level, (axis, bit) in enumerate(bits, start=1):
        own_p[level], other_p[level] = total_p, swap(total_p, axis, bit)
        if level < levels:
            total_p = own_p[level] + other_p[level]

    order = list(chunks)
    keep, send = all_samples(front, tile_mask, place, [chunks[k] for k in order], order)
    got = swap(send, "col", 0)
    slots = {2 * k: (keep[k], got[k]) for k in range(col_count // 2)}
    for bit in range(1, col_levels):
        far = 1 << bit
        left = list(range(0, col_count, 2 * far))
        moved = swap(jnp.stack([slots[k + far][0] + slots[k + far][1] for k in left]), "col", bit)
        slots = {k: (slots[k][0] + slots[k][1], moved[i]) for i, k in enumerate(left)}
    own_a, own_b = slots[0]
    other_a = swap(own_a, "col", 0)
    other_b = swap(own_b, "col", 0)

    leaf_basis, state, send = first_merge(side, (own_a, own_b, other_a, other_b, own_w, other_w))
    buffer = None
    for level, (axis, bit) in list(enumerate(bits, start=1))[1:]:
        near = swap(send, axis, bit)
        far = swap(near, "col", 0)
        buffer, *rest = upper_merge(
            level, levels, side, (state, own_p[level], near, far, other_p[level]), buffer
        )
        if rest:
            state, send = rest
    return (leaf_basis, buffer)


def solution(mesh):
    in_specs = (P("row", "col"), P("row", "col"), P(("col", "row"), None), P(("row", "col"), None))
    out_specs = (P(("row", "col"), None), P(None, ("row", "col"), None))
    return jax.shard_map(step, mesh=mesh, in_specs=in_specs, out_specs=out_specs, check_vma=False)
```

```python
import functools

import jax
import jax.numpy as jnp
from jax import lax
from jax.experimental import pallas as pl
from jax.experimental.pallas import tpu as pltpu
from jax.sharding import PartitionSpec as P

F32 = jnp.float32
BF16 = jnp.bfloat16
SUB, LANE = 8, 128
BLOCK = LANE // 2
PANEL = 2


def split(x):
    high = x.astype(BF16)
    return high, (x - high.astype(F32)).astype(BF16)


def dot(left, right, dims):
    return lax.dot_general(
        left, right, (((dims[0],), (dims[1],)), ((), ())), preferred_element_type=F32
    )


def product(left, right, dims):
    total = None
    for i in reversed(range(len(left))):
        for j in reversed(range(len(right))):
            if i + j < 2:
                term = dot(left[i], right[j], dims)
                total = term if total is None else total + term
    return total


def lane_copy(x, lane):
    return jnp.take_along_axis(
        x, jnp.full(x.shape, lane, jnp.int32), axis=1, mode="promise_in_bounds"
    )


def row_copy(x, row):
    return jnp.broadcast_to(x[row : row + 1, :], x.shape)


def tree_sum(terms):
    while len(terms) > 1:
        pairs = [terms[i] + terms[i + 1] for i in range(0, len(terms) - 1, 2)]
        terms = pairs + terms[len(pairs) * 2 :]
    return terms[0]


def factor_block(packed, offset):
    count = BLOCK // SUB
    rows = [packed[SUB * k : SUB * (k + 1), :] for k in range(count)]
    sub = lax.broadcasted_iota(jnp.int32, (SUB, LANE), 0)
    out = []
    for first in range(0, count, PANEL):
        width, start = SUB * PANEL, offset + SUB * first
        held = rows[first : first + PANEL]
        cols = [[lane_copy(held[q], start + t) for q in range(PANEL)] for t in range(width)]
        done, scales = [None] * PANEL, [None] * PANEL
        for s in range(width):
            own, at = divmod(s, SUB)
            if at == 0:
                for t in range(s, width):
                    for q in range(own):
                        cols[t][q] = lane_copy(held[q], start + t)
            here = sub == at
            pivot = row_copy(cols[s][own], at)
            scale = 1.0 / pivot
            root = lax.rsqrt(pivot)
            bare = [jnp.where(here, 0.0, cols[s][q]) if q == own else cols[s][q] for q in range(PANEL)]
            factor = [x * scale for x in bare]
            row = row_copy(held[own], at)
            if at == 0:
                done[own], scales[own] = row * root, scale
            else:
                done[own] = jnp.where(here, row * root, done[own])
                scales[own] = jnp.where(here, scale, scales[own])
            for t in range(s + 1, width):
                across = row_copy(cols[s][t // SUB], t % SUB)
                for q in range(PANEL):
                    if q < t // SUB and own < t // SUB:
                        continue
                    if t == s + 1:
                        cols[t][q] = cols[t][q] - (bare[q] * across) * scale
                    else:
                        cols[t][q] = cols[t][q] - factor[q] * across
            for q in range(PANEL):
                held[q] = held[q] - factor[q] * row
        out += done
        if first + PANEL < count:
            held = [held[q] * scales[q] for q in range(PANEL)]
            solved = [row_copy(held[s // SUB], s % SUB) for s in range(width)]
            for k in range(first + PANEL, count):
                weight = [lane_copy(rows[k], start + s) for s in range(width)]
                rows[k] = rows[k] - tree_sum([weight[s] * solved[s] for s in range(width)])
    return jnp.concatenate(out, axis=0)


def four(x):
    high, low = split(x)
    return jnp.concatenate([high, high, low, low], axis=0)


def two_parts(x):
    high = x.astype(BF16).astype(F32)
    return high, x - high


def factor_all(gram, rights):
    count = gram.shape[0] // BLOCK
    lane = lax.broadcasted_iota(jnp.int32, (BLOCK, LANE), 1)
    sub = lax.broadcasted_iota(jnp.int32, (BLOCK, LANE), 0)
    blocks = [gram[BLOCK * i : BLOCK * (i + 1), :] for i in range(count)]
    rights = [[x[BLOCK * i : BLOCK * (i + 1), :] for i in range(count)] for x in rights]
    upper, solved = [], [[] for _ in rights]
    for i in range(count):
        first, offset = BLOCK * i // LANE * LANE, BLOCK * i % LANE
        other = BLOCK - offset
        mine = (lane >= offset) & (lane < offset + BLOCK)
        tile = slice(first, first + LANE)
        both = factor_block(
            jnp.where(mine, blocks[i][:, tile], jnp.where(lane - other == sub, 1.0, 0.0)), offset
        )
        high, low = two_parts(jnp.where(mine, 0.0, both))
        low_here = pltpu.roll(low, BLOCK, 1)
        left = jnp.concatenate([jnp.where(mine, low_here, high), high], axis=1).astype(BF16)
        right = [dot(left, four(x[i]), (1, 0)) for x in rights]
        for x, y in zip(solved, right):
            x.append(y)
        row = both
        if i + 1 < count:
            high_here = pltpu.roll(high, BLOCK, 1)
            across = jnp.concatenate([high_here, low_here, high_here], axis=1).astype(BF16)
            below = jnp.concatenate([blocks[j][:, tile] for j in range(i + 1, count)], axis=0)
            high, low = split(below)
            column = dot(
                jnp.concatenate([high, high, low], axis=1),
                jnp.concatenate([across, across], axis=0),
                (1, 1),
            )
            row = dot(left, four(blocks[i][:, first:]), (1, 0))
            high, low = two_parts(column)
            near = lax.broadcasted_iota(jnp.int32, column.shape, 1) < BLOCK
            column = jnp.concatenate(
                [jnp.where(near, high, low), jnp.where(near, high, 0.0)], axis=1
            ).astype(BF16)
            change = dot(column, four(row), (1, 0))
            for j in range(i + 1, count):
                at = BLOCK * (j - i - 1)
                new = blocks[j][:, first:] - change[at : at + BLOCK, :]
                if first:
                    new = jnp.concatenate([blocks[j][:, :first], new], axis=1)
                blocks[j] = new
            for x, y in zip(rights, right):
                change = dot(column, four(y), (1, 0))
                for j in range(i + 1, count):
                    at = BLOCK * (j - i - 1)
                    x[j] = x[j] - change[at : at + BLOCK, :]
        head = jnp.where(mine, both, row[:, :LANE])
        head = jnp.where(lane < offset + jnp.where(mine, sub, 0), 0.0, head)
        upper.append(head if row.shape[1] == LANE else jnp.concatenate([head, row[:, LANE:]], axis=1))
    return upper, [jnp.concatenate(x, axis=0) for x in solved]


def merge_math(own, other, level, want_state):
    own_s, own_w, own_p = own
    other_s, other_w, other_p = other
    if level > 1:
        factor = 2.0 ** (-(level - 1) / 2.0)
        own_s = own_s - factor * product(own_p, other_w, (1, 0))
        other_s = other_s - factor * product(other_p, own_w, (1, 0))
    size = own_s.shape[1]
    own_h, other_h = split(own_s), split(other_s)
    gram = product(own_h, own_h, (0, 0)) + product(other_h, other_h, (0, 0))
    trace = jnp.sum(own_s * own_s) + jnp.sum(other_s * other_s)
    shift = 0.001 * (trace / size + 1e-06)
    eye = lax.broadcasted_iota(jnp.int32, (size, size), 0) == lax.broadcasted_iota(
        jnp.int32, (size, size), 1
    )
    rights = [jnp.where(eye, 1.0, 0.0)]
    if want_state:
        rights.append(product(own_h, own_w, (0, 0)) + product(other_h, other_w, (0, 0)))
    upper, solved = factor_all(gram + jnp.where(eye, shift, 0.0), rights)
    q = product(own_h, split(solved[0]), (1, 1))
    return q, upper, solved[1] if want_state else None


def store_state(side, upper, w, state, send):
    half = w.shape[0] // 2
    part = half // 2
    share = half - part // 2
    state[0, :half] = w[:half]
    state[1, :half] = w[half:]
    top = jnp.concatenate(upper[:2], axis=0)
    state[0, half:] = top[:share]
    state[1, half : half + half - share] = top[share:]
    state[1, half + half - share :] = jnp.concatenate(upper[2:], axis=1)
    send[...] = state[side[0]]


def load_state(first, second):
    half = first.shape[1] // 2
    part = half // 2
    share = half - part // 2
    w = jnp.concatenate([first[:half], second[:half]], axis=0)
    split_at = half + half - share
    top = jnp.concatenate([first[half:], second[half:split_at]], axis=0)
    last = second[split_at:]
    corner = jnp.concatenate([last[:, :half], last[:, half:]], axis=0)
    bottom = jnp.concatenate([jnp.zeros((half, half), F32), corner], axis=1)
    return jnp.concatenate([top, bottom], axis=0), w


def first_kernel(
    side, own_a, own_b, other_a, other_b, own_w, other_w, q_out, state, send
):
    q, upper, w = merge_math(
        (own_a[...] + own_b[...], (own_w[...],), None),
        (other_a[...] + other_b[...], (other_w[...],), None),
        1,
        True,
    )
    store_state(side, upper, w, state, send)
    q_out[...] = q


def upper_kernel(level, is_last, has_buffer, side, own, own_p, near, far, other_p, *refs):
    refs = list(refs)
    if has_buffer:
        refs.pop(0)
    q_all = refs.pop(0)
    outs = [] if is_last else [refs.pop(0), refs.pop(0)]
    q_here, done = refs
    is_first = side[0] == 0
    own_s, own_w = load_state(own[0], own[1])
    near, far = near[...], far[...]
    other_s, other_w = load_state(jnp.where(is_first, near, far), jnp.where(is_first, far, near))
    q, upper, w = merge_math(
        (own_s, split(own_w), split(own_p[...])),
        (other_s, split(other_w), split(other_p[...])),
        level,
        not is_last,
    )
    q_here[...] = q
    copy = pltpu.make_async_copy(q_here, q_all.at[level - 2], done)
    copy.start()
    if not is_last:
        store_state(side, upper, w, *outs)
    copy.wait()


VMEM = pl.BlockSpec(memory_space=pltpu.VMEM)
SMEM = pl.BlockSpec(memory_space=pltpu.SMEM)
ANY = pl.BlockSpec(memory_space=pl.ANY)


def near_core(arrays):
    return [pltpu.with_memory_space_constraint(x, pltpu.VMEM) for x in arrays]


def state_shapes(size):
    rows = size // 2 + 3 * size // 8
    return [pltpu.VMEM((2, rows, size), F32), pltpu.VMEM((rows, size), F32)]


def first_merge(side, arrays):
    rows, size = arrays[0].shape
    return pl.pallas_call(
        first_kernel,
        out_shape=[jax.ShapeDtypeStruct((rows, size), F32)] + state_shapes(size),
        in_specs=[SMEM] + [VMEM] * len(arrays),
        out_specs=[VMEM] * 3,
        name="first_merge",
    )(side, *near_core(arrays))


def upper_merge(level, levels, side, arrays, buffer):
    size = arrays[1].shape[1]
    is_last = level == levels
    extra = [] if buffer is None else [buffer]
    out_shape = [jax.ShapeDtypeStruct((levels - 1, size, size), F32)]
    out_shape += [] if is_last else state_shapes(size)
    return pl.pallas_call(
        functools.partial(upper_kernel, level, is_last, bool(extra)),
        out_shape=out_shape,
        in_specs=[SMEM] + [VMEM] * len(arrays) + [ANY] * len(extra),
        out_specs=[ANY] + [VMEM] * (len(out_shape) - 1),
        scratch_shapes=[pltpu.VMEM((size, size), F32), pltpu.SemaphoreType.DMA(())],
        input_output_aliases={1 + len(arrays): 0} if extra else {},
    )(side, *near_core(arrays), *extra)


def sample_kernel(keys, place, mask, front, *refs):
    count = len(keys)
    chunks, (keep, send, tiles, arrived) = refs[:count], refs[count:]
    leaf = chunks[0].shape[0]
    slots = 2 * keep.shape[0]
    order = [*range(1, slots, 2), *range(0, slots, 2)]
    present, copies = {}, {}
    for slot in order:
        tile_row = place[1] ^ slot
        for j, key in enumerate(keys):
            chunk = place[0] ^ key
            row_tile = place[0] * slots + tile_row
            col_tile = place[1] * count + chunk
            present[slot, j] = (mask[tile_row, chunk] != 0) & (row_tile // 2 != col_tile // 2)
            copies[slot, j] = pltpu.make_async_copy(
                front.at[
                    pl.ds(pl.multiple_of(tile_row * leaf, leaf), leaf),
                    pl.ds(pl.multiple_of(chunk * leaf, leaf), leaf),
                ],
                tiles.at[slot, j],
                arrived.at[slot, j],
            )

            @pl.when(present[slot, j])
            def _():
                copies[slot, j].start()

    probes = jnp.concatenate([x[...] for x in chunks], axis=0)
    for slot in order:
        for j in range(count):

            @pl.when(present[slot, j])
            def _():
                copies[slot, j].wait()

        row = [
            jnp.where(present[slot, j], tiles[slot, j], jnp.zeros((), BF16)) for j in range(count)
        ]
        out = send if slot % 2 else keep
        out[slot // 2] = dot(jnp.concatenate(row, axis=1), probes, (1, 0))


def all_samples(front, tile_mask, place, chunks, keys):
    leaf, size = chunks[0].shape
    slots = front.shape[0] // leaf
    small = len(keys) * leaf * size < 2**20
    return pl.pallas_call(
        functools.partial(sample_kernel, keys),
        out_shape=[(pltpu.VMEM if small else jax.ShapeDtypeStruct)((slots // 2, leaf, size), F32)] * 2,
        in_specs=[SMEM, SMEM, ANY] + [VMEM] * len(keys),
        out_specs=[VMEM] * 2,
        scratch_shapes=[
            pltpu.VMEM((slots, len(keys), leaf, leaf), BF16),
            pltpu.SemaphoreType.DMA((slots, len(keys))),
        ],
        name="samples",
    )(place, tile_mask, front, *(near_core(chunks) if small else chunks))


def swap(x, axis, bit):
    return lax.ppermute(x, axis, [(i, i ^ (1 << bit)) for i in range(lax.axis_size(axis))])


def step(front, tile_mask, probes, coupling):
    col_count, row_count = lax.axis_size("col"), lax.axis_size("row")
    row_index, col_index = lax.axis_index("row"), lax.axis_index("col")
    col_levels, row_levels = col_count.bit_length() - 1, row_count.bit_length() - 1
    levels = col_levels + row_levels
    place = jnp.stack([row_index, col_index]).astype(jnp.int32)
    side = (col_index & 1).astype(jnp.int32)[None]
    bits = [("col", b) for b in range(col_levels)] + [("row", b) for b in range(row_levels)]

    chunks = {0: probes}
    chunks[1] = swap(probes, "row", 0)
    for bit in range(row_levels - 1, 0, -1):
        for key in list(chunks):
            new = key | 1 << bit
            if key == 1:
                chunks[new] = swap(chunks[new ^ 1], "row", 0)
            else:
                chunks[new] = swap(chunks[key], "row", bit)

    pairs = [
        ((b % row_count) * col_count + b // row_count, b) for b in range(row_count * col_count)
    ]
    own_w = lax.ppermute(probes, ("row", "col"), pairs)
    other_w = swap(own_w, "col", 0)

    own_p, other_p, total_p = {}, {}, coupling
    for level, (axis, bit) in enumerate(bits, start=1):
        own_p[level], other_p[level] = total_p, swap(total_p, axis, bit)
        if level < levels:
            total_p = own_p[level] + other_p[level]

    order = list(chunks)
    keep, send = all_samples(front, tile_mask, place, [chunks[k] for k in order], order)
    got = swap(send, "col", 0)
    slots = {2 * k: (keep[k], got[k]) for k in range(col_count // 2)}
    for bit in range(1, col_levels):
        far = 1 << bit
        left = list(range(0, col_count, 2 * far))
        moved = swap(jnp.stack([slots[k + far][0] + slots[k + far][1] for k in left]), "col", bit)
        slots = {k: (slots[k][0] + slots[k][1], moved[i]) for i, k in enumerate(left)}
    own_a, own_b = slots[0]
    other_a = swap(own_a, "col", 0)
    other_b = swap(own_b, "col", 0)

    leaf_basis, state, send = first_merge(
        side, (own_a, own_b, other_a, other_b, own_w, other_w)
    )
    buffer = None
    for level, (axis, bit) in list(enumerate(bits, start=1))[1:]:
        near = swap(send, axis, bit)
        far = swap(near, "col", 0)
        buffer, *rest = upper_merge(
            level, levels, side, (state, own_p[level], near, far, other_p[level]), buffer
        )
        if rest:
            state, send = rest
    return (leaf_basis, buffer)


def solution(mesh):
    in_specs = (P("row", "col"), P("row", "col"), P(("col", "row"), None), P(("row", "col"), None))
    out_specs = (P(("row", "col"), None), P(None, ("row", "col"), None))
    return jax.shard_map(step, mesh=mesh, in_specs=in_specs, out_specs=out_specs, check_vma=False)
```

```python
import functools

import jax
import jax.numpy as jnp
from jax import lax
from jax.experimental import pallas as pl
from jax.experimental.pallas import tpu as pltpu
from jax.sharding import PartitionSpec as P

F32 = jnp.float32
BF16 = jnp.bfloat16
SUB, LANE = 8, 128
BLOCK = LANE // 2
PANEL = 2
SCRATCH_BYTES = 16 * 2**20


def split(x):
    high = x.astype(BF16)
    return high, (x - high.astype(F32)).astype(BF16)


def dot(left, right, dims):
    return lax.dot_general(
        left, right, (((dims[0],), (dims[1],)), ((), ())), preferred_element_type=F32
    )


def product(left, right, dims):
    total = None
    for i in reversed(range(len(left))):
        for j in reversed(range(len(right))):
            if i + j < 2:
                term = dot(left[i], right[j], dims)
                total = term if total is None else total + term
    return total


def lane_copy(x, lane):
    return jnp.take_along_axis(
        x, jnp.full(x.shape, lane, jnp.int32), axis=1, mode="promise_in_bounds"
    )


def row_copy(x, row):
    return jnp.broadcast_to(x[row : row + 1, :], x.shape)


def tree_sum(terms):
    while len(terms) > 1:
        pairs = [terms[i] + terms[i + 1] for i in range(0, len(terms) - 1, 2)]
        terms = pairs + terms[len(pairs) * 2 :]
    return terms[0]


def factor_block(packed, offset):
    count = BLOCK // SUB
    rows = [packed[SUB * k : SUB * (k + 1), :] for k in range(count)]
    sub = lax.broadcasted_iota(jnp.int32, (SUB, LANE), 0)
    out = []
    for first in range(0, count, PANEL):
        width, start = SUB * PANEL, offset + SUB * first
        held = rows[first : first + PANEL]
        cols = [[lane_copy(held[q], start + t) for q in range(PANEL)] for t in range(width)]
        done, scales = [None] * PANEL, [None] * PANEL
        for s in range(width):
            own, at = divmod(s, SUB)
            if at == 0:
                for t in range(s, width):
                    for q in range(own):
                        cols[t][q] = lane_copy(held[q], start + t)
            here = sub == at
            pivot = row_copy(cols[s][own], at)
            scale = 1.0 / pivot
            root = lax.rsqrt(pivot)
            bare = [jnp.where(here, 0.0, cols[s][q]) if q == own else cols[s][q] for q in range(PANEL)]
            factor = [x * scale for x in bare]
            row = row_copy(held[own], at)
            if at == 0:
                done[own], scales[own] = row * root, scale
            else:
                done[own] = jnp.where(here, row * root, done[own])
                scales[own] = jnp.where(here, scale, scales[own])
            for t in range(s + 1, width):
                across = row_copy(cols[s][t // SUB], t % SUB)
                for q in range(PANEL):
                    if q < t // SUB and own < t // SUB:
                        continue
                    if t == s + 1:
                        cols[t][q] = cols[t][q] - (bare[q] * across) * scale
                    else:
                        cols[t][q] = cols[t][q] - factor[q] * across
            for q in range(PANEL):
                held[q] = held[q] - factor[q] * row
        out += done
        if first + PANEL < count:
            held = [held[q] * scales[q] for q in range(PANEL)]
            solved = [row_copy(held[s // SUB], s % SUB) for s in range(width)]
            for k in range(first + PANEL, count):
                weight = [lane_copy(rows[k], start + s) for s in range(width)]
                rows[k] = rows[k] - tree_sum([weight[s] * solved[s] for s in range(width)])
    return jnp.concatenate(out, axis=0)


def four(x):
    high, low = split(x)
    return jnp.concatenate([high, high, low, low], axis=0)


def two_parts(x):
    high = x.astype(BF16).astype(F32)
    return high, x - high


def factor_all(gram, rights):
    count = gram.shape[0] // BLOCK
    lane = lax.broadcasted_iota(jnp.int32, (BLOCK, LANE), 1)
    sub = lax.broadcasted_iota(jnp.int32, (BLOCK, LANE), 0)
    blocks = [gram[BLOCK * i : BLOCK * (i + 1), :] for i in range(count)]
    rights = [[x[BLOCK * i : BLOCK * (i + 1), :] for i in range(count)] for x in rights]
    upper, solved = [], [[] for _ in rights]
    for i in range(count):
        first, offset = BLOCK * i // LANE * LANE, BLOCK * i % LANE
        other = BLOCK - offset
        mine = (lane >= offset) & (lane < offset + BLOCK)
        tile = slice(first, first + LANE)
        both = factor_block(
            jnp.where(mine, blocks[i][:, tile], jnp.where(lane - other == sub, 1.0, 0.0)), offset
        )
        high, low = two_parts(jnp.where(mine, 0.0, both))
        low_here = pltpu.roll(low, BLOCK, 1)
        left = jnp.concatenate([jnp.where(mine, low_here, high), high], axis=1).astype(BF16)
        right = [dot(left, four(x[i]), (1, 0)) for x in rights]
        for x, y in zip(solved, right):
            x.append(y)
        row = both
        if i + 1 < count:
            high_here = pltpu.roll(high, BLOCK, 1)
            across = jnp.concatenate([high_here, low_here, high_here], axis=1).astype(BF16)
            below = jnp.concatenate([blocks[j][:, tile] for j in range(i + 1, count)], axis=0)
            high, low = split(below)
            column = dot(
                jnp.concatenate([high, high, low], axis=1),
                jnp.concatenate([across, across], axis=0),
                (1, 1),
            )
            row = dot(left, four(blocks[i][:, first:]), (1, 0))
            high, low = two_parts(column)
            near = lax.broadcasted_iota(jnp.int32, column.shape, 1) < BLOCK
            column = jnp.concatenate(
                [jnp.where(near, high, low), jnp.where(near, high, 0.0)], axis=1
            ).astype(BF16)
            change = dot(column, four(row), (1, 0))
            for j in range(i + 1, count):
                at = BLOCK * (j - i - 1)
                new = blocks[j][:, first:] - change[at : at + BLOCK, :]
                if first:
                    new = jnp.concatenate([blocks[j][:, :first], new], axis=1)
                blocks[j] = new
            for x, y in zip(rights, right):
                change = dot(column, four(y), (1, 0))
                for j in range(i + 1, count):
                    at = BLOCK * (j - i - 1)
                    x[j] = x[j] - change[at : at + BLOCK, :]
        head = jnp.where(mine, both, row[:, :LANE])
        head = jnp.where(lane < offset + jnp.where(mine, sub, 0), 0.0, head)
        upper.append(head if row.shape[1] == LANE else jnp.concatenate([head, row[:, LANE:]], axis=1))
    return upper, [jnp.concatenate(x, axis=0) for x in solved]


def merge_math(own, other, level, want_state):
    own_s, own_w, own_p = own
    other_s, other_w, other_p = other
    if level > 1:
        factor = 2.0 ** (-(level - 1) / 2.0)
        own_s = own_s - factor * product(own_p, other_w, (1, 0))
        other_s = other_s - factor * product(other_p, own_w, (1, 0))
    size = own_s.shape[1]
    own_h, other_h = split(own_s), split(other_s)
    gram = product(own_h, own_h, (0, 0)) + product(other_h, other_h, (0, 0))
    trace = jnp.sum(own_s * own_s) + jnp.sum(other_s * other_s)
    shift = 0.001 * (trace / size + 1e-06)
    eye = lax.broadcasted_iota(jnp.int32, (size, size), 0) == lax.broadcasted_iota(
        jnp.int32, (size, size), 1
    )
    rights = [jnp.where(eye, 1.0, 0.0)]
    if want_state:
        rights.append(product(own_h, own_w, (0, 0)) + product(other_h, other_w, (0, 0)))
    upper, solved = factor_all(gram + jnp.where(eye, shift, 0.0), rights)
    q = product(own_h, split(solved[0]), (1, 1))
    return q, upper, solved[1] if want_state else None


def store_state(side, upper, w, state, send):
    half = w.shape[0] // 2
    part = half // 2
    share = half - part // 2
    state[0, :half] = w[:half]
    state[1, :half] = w[half:]
    top = jnp.concatenate(upper[:2], axis=0)
    state[0, half:] = top[:share]
    state[1, half : half + half - share] = top[share:]
    state[1, half + half - share :] = jnp.concatenate(upper[2:], axis=1)
    send[...] = state[side[0]]


def load_state(first, second):
    half = first.shape[1] // 2
    part = half // 2
    share = half - part // 2
    w = jnp.concatenate([first[:half], second[:half]], axis=0)
    split_at = half + half - share
    top = jnp.concatenate([first[half:], second[half:split_at]], axis=0)
    last = second[split_at:]
    corner = jnp.concatenate([last[:, :half], last[:, half:]], axis=0)
    bottom = jnp.concatenate([jnp.zeros((half, half), F32), corner], axis=1)
    return jnp.concatenate([top, bottom], axis=0), w


def first_kernel(
    side, own_a, own_b, other_a, other_b, own_w, other_w, q_out, state, send
):
    q, upper, w = merge_math(
        (own_a[...] + own_b[...], (own_w[...],), None),
        (other_a[...] + other_b[...], (other_w[...],), None),
        1,
        True,
    )
    store_state(side, upper, w, state, send)
    q_out[...] = q


def upper_kernel(level, is_last, has_buffer, side, own, own_p, near, far, other_p, *refs):
    refs = list(refs)
    if has_buffer:
        refs.pop(0)
    q_all = refs.pop(0)
    outs = [] if is_last else [refs.pop(0), refs.pop(0)]
    q_here, done = refs
    is_first = side[0] == 0
    own_s, own_w = load_state(own[0], own[1])
    near, far = near[...], far[...]
    other_s, other_w = load_state(jnp.where(is_first, near, far), jnp.where(is_first, far, near))
    q, upper, w = merge_math(
        (own_s, split(own_w), split(own_p[...])),
        (other_s, split(other_w), split(other_p[...])),
        level,
        not is_last,
    )
    q_here[...] = q
    copy = pltpu.make_async_copy(q_here, q_all.at[level - 2], done)
    copy.start()
    if not is_last:
        store_state(side, upper, w, *outs)
    copy.wait()


VMEM = pl.BlockSpec(memory_space=pltpu.VMEM)
SMEM = pl.BlockSpec(memory_space=pltpu.SMEM)
ANY = pl.BlockSpec(memory_space=pl.ANY)


def near_core(arrays):
    return [pltpu.with_memory_space_constraint(x, pltpu.VMEM) for x in arrays]


def state_shapes(size):
    rows = size // 2 + 3 * size // 8
    return [pltpu.VMEM((2, rows, size), F32), pltpu.VMEM((rows, size), F32)]


def first_merge(side, arrays):
    rows, size = arrays[0].shape
    return pl.pallas_call(
        first_kernel,
        out_shape=[jax.ShapeDtypeStruct((rows, size), F32)] + state_shapes(size),
        in_specs=[SMEM] + [VMEM] * len(arrays),
        out_specs=[VMEM] * 3,
        compiler_params=pltpu.CompilerParams(vmem_limit_bytes=SCRATCH_BYTES),
        name="first_merge",
    )(side, *near_core(arrays))


def upper_merge(level, levels, side, arrays, buffer):
    size = arrays[1].shape[1]
    is_last = level == levels
    extra = [] if buffer is None else [buffer]
    out_shape = [jax.ShapeDtypeStruct((levels - 1, size, size), F32)]
    out_shape += [] if is_last else state_shapes(size)
    return pl.pallas_call(
        functools.partial(upper_kernel, level, is_last, bool(extra)),
        out_shape=out_shape,
        in_specs=[SMEM] + [VMEM] * len(arrays) + [ANY] * len(extra),
        out_specs=[ANY] + [VMEM] * (len(out_shape) - 1),
        scratch_shapes=[pltpu.VMEM((size, size), F32), pltpu.SemaphoreType.DMA(())],
        input_output_aliases={1 + len(arrays): 0} if extra else {},
        compiler_params=pltpu.CompilerParams(vmem_limit_bytes=SCRATCH_BYTES),
    )(side, *near_core(arrays), *extra)


def load_kernel(keys, place, mask, front, own, rows, own_here, arrived):
    slots, leaf = rows.shape[:2]
    own_copy = pltpu.make_async_copy(own, own_here, arrived.at[slots, 0])
    own_copy.start()
    tiles = []
    for slot in range(slots):
        for j, key in enumerate(keys):
            tile_row, chunk = place[1] ^ slot, place[0] ^ key
            row_tile = place[0] * slots + tile_row
            col_tile = place[1] * len(keys) + chunk
            present = (mask[tile_row, chunk] != 0) & (row_tile // 2 != col_tile // 2)
            here = rows.at[slot, :, pl.ds(j * leaf, leaf)]
            copy = pltpu.make_async_copy(
                front.at[
                    pl.ds(pl.multiple_of(tile_row * leaf, leaf), leaf),
                    pl.ds(pl.multiple_of(chunk * leaf, leaf), leaf),
                ],
                here,
                arrived.at[slot, j],
            )
            tiles.append((present, copy))

            @pl.when(present)
            def _():
                copy.start()

            @pl.when(jnp.logical_not(present))
            def _():
                here[...] = jnp.zeros(here.shape, BF16)

    for present, copy in tiles:

        @pl.when(present)
        def _():
            copy.wait()

    own_copy.wait()


def load_front(front, tile_mask, place, own, keys):
    leaf, size = own.shape
    slots, width = front.shape[0] // leaf, front.shape[1]
    small = width * size < 2**20
    form = pltpu.VMEM if small else jax.ShapeDtypeStruct
    return pl.pallas_call(
        functools.partial(load_kernel, keys),
        out_shape=[form((slots, leaf, width), BF16), form((leaf, size), BF16)],
        in_specs=[SMEM, SMEM, ANY, ANY],
        out_specs=[VMEM] * 2,
        scratch_shapes=[pltpu.SemaphoreType.DMA((slots + 1, len(keys)))],
        compiler_params=pltpu.CompilerParams(vmem_limit_bytes=SCRATCH_BYTES * (1 if small else 3)),
        name="load_front",
    )(
        place,
        tile_mask,
        pltpu.with_memory_space_constraint(front, pltpu.HBM),
        pltpu.with_memory_space_constraint(own, pltpu.HBM),
    )


def sample_kernel(rows, *refs):
    chunks, (keep, send) = refs[:-2], refs[-2:]
    slots = rows.shape[0]
    probes = jnp.concatenate([x[...] for x in chunks], axis=0)
    for slot in [*range(1, slots, 2), *range(0, slots, 2)]:
        out = send if slot % 2 else keep
        out[slot // 2] = dot(rows[slot], probes, (1, 0))


def all_samples(rows, chunks):
    slots, leaf, width = rows.shape
    size = chunks[0].shape[1]
    small = width * size < 2**20
    form = pltpu.VMEM if small else jax.ShapeDtypeStruct
    arrays = [rows, *chunks]
    return pl.pallas_call(
        sample_kernel,
        out_shape=[form((slots // 2, leaf, size), F32)] * 2,
        in_specs=[VMEM] * len(arrays),
        out_specs=[VMEM] * 2,
        compiler_params=pltpu.CompilerParams(vmem_limit_bytes=SCRATCH_BYTES * (1 if small else 3)),
        name="samples",
    )(*(near_core(arrays) if small else arrays))


def swap(x, axis, bit):
    return lax.ppermute(x, axis, [(i, i ^ (1 << bit)) for i in range(lax.axis_size(axis))])


def step(front, tile_mask, probes, coupling):
    col_count, row_count = lax.axis_size("col"), lax.axis_size("row")
    row_index, col_index = lax.axis_index("row"), lax.axis_index("col")
    col_levels, row_levels = col_count.bit_length() - 1, row_count.bit_length() - 1
    levels = col_levels + row_levels
    place = jnp.stack([row_index, col_index]).astype(jnp.int32)
    side = (col_index & 1).astype(jnp.int32)[None]
    bits = [("col", b) for b in range(col_levels)] + [("row", b) for b in range(row_levels)]

    chunks = {0: probes}
    chunks[1] = swap(probes, "row", 0)
    for bit in range(row_levels - 1, 0, -1):
        for key in list(chunks):
            new = key | 1 << bit
            if key == 1:
                chunks[new] = swap(chunks[new ^ 1], "row", 0)
            else:
                chunks[new] = swap(chunks[key], "row", bit)

    pairs = [
        ((b % row_count) * col_count + b // row_count, b) for b in range(row_count * col_count)
    ]
    own_w = lax.ppermute(probes, ("row", "col"), pairs)
    other_w = swap(own_w, "col", 0)

    own_p, other_p, total_p = {}, {}, coupling
    for level, (axis, bit) in enumerate(bits, start=1):
        own_p[level], other_p[level] = total_p, swap(total_p, axis, bit)
        if level < levels:
            total_p = own_p[level] + other_p[level]

    order = list(chunks)
    rows, own_chunk = load_front(front, tile_mask, place, probes, order)
    keep, send = all_samples(rows, [own_chunk] + [chunks[k] for k in order[1:]])
    got = swap(send, "col", 0)
    slots = {2 * k: (keep[k], got[k]) for k in range(col_count // 2)}
    for bit in range(1, col_levels):
        far = 1 << bit
        left = list(range(0, col_count, 2 * far))
        moved = swap(jnp.stack([slots[k + far][0] + slots[k + far][1] for k in left]), "col", bit)
        slots = {k: (slots[k][0] + slots[k][1], moved[i]) for i, k in enumerate(left)}
    own_a, own_b = slots[0]
    other_a = swap(own_a, "col", 0)
    other_b = swap(own_b, "col", 0)

    leaf_basis, state, send = first_merge(
        side, (own_a, own_b, other_a, other_b, own_w, other_w)
    )
    buffer = None
    for level, (axis, bit) in list(enumerate(bits, start=1))[1:]:
        near = swap(send, axis, bit)
        far = swap(near, "col", 0)
        buffer, *rest = upper_merge(
            level, levels, side, (state, own_p[level], near, far, other_p[level]), buffer
        )
        if rest:
            state, send = rest
    return (leaf_basis, buffer)


def solution(mesh):
    in_specs = (P("row", "col"), P("row", "col"), P(("col", "row"), None), P(("row", "col"), None))
    out_specs = (P(("row", "col"), None), P(None, ("row", "col"), None))
    return jax.shard_map(step, mesh=mesh, in_specs=in_specs, out_specs=out_specs, check_vma=False)
```

```python
import functools

import jax
import jax.numpy as jnp
from jax import lax
from jax.experimental import pallas as pl
from jax.experimental.pallas import tpu as pltpu
from jax.sharding import PartitionSpec as P

F32 = jnp.float32
BF16 = jnp.bfloat16
SUB, LANE = 8, 128
BLOCK = LANE // 2
PANEL = 2
SCRATCH_BYTES = 16 * 2**20


def split(x):
    high = x.astype(BF16)
    return high, (x - high.astype(F32)).astype(BF16)


def dot(left, right, dims):
    return lax.dot_general(
        left, right, (((dims[0],), (dims[1],)), ((), ())), preferred_element_type=F32
    )


def product(left, right, dims):
    total = None
    for i in reversed(range(len(left))):
        for j in reversed(range(len(right))):
            if i + j < 2:
                term = dot(left[i], right[j], dims)
                total = term if total is None else total + term
    return total


def lane_copy(x, lane):
    return jnp.take_along_axis(
        x, jnp.full(x.shape, lane, jnp.int32), axis=1, mode="promise_in_bounds"
    )


def row_copy(x, row):
    return jnp.broadcast_to(x[row : row + 1, :], x.shape)


def tree_sum(terms):
    while len(terms) > 1:
        pairs = [terms[i] + terms[i + 1] for i in range(0, len(terms) - 1, 2)]
        terms = pairs + terms[len(pairs) * 2 :]
    return terms[0]


def factor_block(packed, offset):
    count = BLOCK // SUB
    rows = [packed[SUB * k : SUB * (k + 1), :] for k in range(count)]
    sub = lax.broadcasted_iota(jnp.int32, (SUB, LANE), 0)
    out = []
    for first in range(0, count, PANEL):
        width, start = SUB * PANEL, offset + SUB * first
        held = rows[first : first + PANEL]
        cols = [[lane_copy(held[q], start + t) for q in range(PANEL)] for t in range(width)]
        done, scales = [None] * PANEL, [None] * PANEL
        for s in range(width):
            own, at = divmod(s, SUB)
            if at == 0:
                for t in range(s, width):
                    for q in range(own):
                        cols[t][q] = lane_copy(held[q], start + t)
            here = sub == at
            pivot = row_copy(cols[s][own], at)
            scale = 1.0 / pivot
            root = lax.rsqrt(pivot)
            bare = [jnp.where(here, 0.0, cols[s][q]) if q == own else cols[s][q] for q in range(PANEL)]
            factor = [x * scale for x in bare]
            row = row_copy(held[own], at)
            if at == 0:
                done[own], scales[own] = row * root, scale
            else:
                done[own] = jnp.where(here, row * root, done[own])
                scales[own] = jnp.where(here, scale, scales[own])
            for t in range(s + 1, width):
                across = row_copy(cols[s][t // SUB], t % SUB)
                for q in range(PANEL):
                    if q < t // SUB and own < t // SUB:
                        continue
                    if t == s + 1:
                        cols[t][q] = cols[t][q] - (bare[q] * across) * scale
                    else:
                        cols[t][q] = cols[t][q] - factor[q] * across
            for q in range(PANEL):
                held[q] = held[q] - factor[q] * row
        out += done
        if first + PANEL < count:
            held = [held[q] * scales[q] for q in range(PANEL)]
            solved = [row_copy(held[s // SUB], s % SUB) for s in range(width)]
            for k in range(first + PANEL, count):
                weight = [lane_copy(rows[k], start + s) for s in range(width)]
                rows[k] = rows[k] - tree_sum([weight[s] * solved[s] for s in range(width)])
    return jnp.concatenate(out, axis=0)


def four(x):
    high, low = split(x)
    return jnp.concatenate([high, high, low, low], axis=0)


def two_parts(x):
    high = x.astype(BF16).astype(F32)
    return high, x - high


def factor_all(gram, rights):
    count = gram.shape[0] // BLOCK
    lane = lax.broadcasted_iota(jnp.int32, (BLOCK, LANE), 1)
    sub = lax.broadcasted_iota(jnp.int32, (BLOCK, LANE), 0)
    blocks = [gram[BLOCK * i : BLOCK * (i + 1), :] for i in range(count)]
    rights = [[x[BLOCK * i : BLOCK * (i + 1), :] for i in range(count)] for x in rights]
    upper, solved = [], [[] for _ in rights]
    for i in range(count):
        first, offset = BLOCK * i // LANE * LANE, BLOCK * i % LANE
        other = BLOCK - offset
        mine = (lane >= offset) & (lane < offset + BLOCK)
        tile = slice(first, first + LANE)
        both = factor_block(
            jnp.where(mine, blocks[i][:, tile], jnp.where(lane - other == sub, 1.0, 0.0)), offset
        )
        high, low = two_parts(jnp.where(mine, 0.0, both))
        low_here = pltpu.roll(low, BLOCK, 1)
        left = jnp.concatenate([jnp.where(mine, low_here, high), high], axis=1).astype(BF16)
        right = [dot(left, four(x[i]), (1, 0)) for x in rights]
        for x, y in zip(solved, right):
            x.append(y)
        row = both
        if i + 1 < count:
            high_here = pltpu.roll(high, BLOCK, 1)
            across = jnp.concatenate([high_here, low_here, high_here], axis=1).astype(BF16)
            below = jnp.concatenate([blocks[j][:, tile] for j in range(i + 1, count)], axis=0)
            high, low = split(below)
            column = dot(
                jnp.concatenate([high, high, low], axis=1),
                jnp.concatenate([across, across], axis=0),
                (1, 1),
            )
            row = dot(left, four(blocks[i][:, first:]), (1, 0))
            high, low = two_parts(column)
            near = lax.broadcasted_iota(jnp.int32, column.shape, 1) < BLOCK
            column = jnp.concatenate(
                [jnp.where(near, high, low), jnp.where(near, high, 0.0)], axis=1
            ).astype(BF16)
            change = dot(column, four(row), (1, 0))
            for j in range(i + 1, count):
                at = BLOCK * (j - i - 1)
                new = blocks[j][:, first:] - change[at : at + BLOCK, :]
                if first:
                    new = jnp.concatenate([blocks[j][:, :first], new], axis=1)
                blocks[j] = new
            for x, y in zip(rights, right):
                change = dot(column, four(y), (1, 0))
                for j in range(i + 1, count):
                    at = BLOCK * (j - i - 1)
                    x[j] = x[j] - change[at : at + BLOCK, :]
        head = jnp.where(mine, both, row[:, :LANE])
        head = jnp.where(lane < offset + jnp.where(mine, sub, 0), 0.0, head)
        upper.append(head if row.shape[1] == LANE else jnp.concatenate([head, row[:, LANE:]], axis=1))
    return upper, [jnp.concatenate(x, axis=0) for x in solved]


def merge_math(own, other, level, want_state):
    own_s, own_w, own_p = own
    other_s, other_w, other_p = other
    if level > 1:
        factor = 2.0 ** (-(level - 1) / 2.0)
        own_s = own_s - factor * product(own_p, other_w, (1, 0))
        other_s = other_s - factor * product(other_p, own_w, (1, 0))
    size = own_s.shape[1]
    own_h, other_h = split(own_s), split(other_s)
    gram = product(own_h, own_h, (0, 0)) + product(other_h, other_h, (0, 0))
    trace = jnp.sum(own_s * own_s) + jnp.sum(other_s * other_s)
    shift = 0.001 * (trace / size + 1e-06)
    eye = lax.broadcasted_iota(jnp.int32, (size, size), 0) == lax.broadcasted_iota(
        jnp.int32, (size, size), 1
    )
    rights = [jnp.where(eye, 1.0, 0.0)]
    if want_state:
        rights.append(product(own_h, own_w, (0, 0)) + product(other_h, other_w, (0, 0)))
    upper, solved = factor_all(gram + jnp.where(eye, shift, 0.0), rights)
    q = product(own_h, split(solved[0]), (1, 1))
    return q, upper, solved[1] if want_state else None


def store_state(side, upper, w, state, send):
    half = w.shape[0] // 2
    part = half // 2
    share = half - part // 2
    state[0, :half] = w[:half]
    state[1, :half] = w[half:]
    top = jnp.concatenate(upper[:2], axis=0)
    state[0, half:] = top[:share]
    state[1, half : half + half - share] = top[share:]
    state[1, half + half - share :] = jnp.concatenate(upper[2:], axis=1)
    send[...] = state[side[0]]


def load_state(first, second):
    half = first.shape[1] // 2
    part = half // 2
    share = half - part // 2
    w = jnp.concatenate([first[:half], second[:half]], axis=0)
    split_at = half + half - share
    top = jnp.concatenate([first[half:], second[half:split_at]], axis=0)
    last = second[split_at:]
    corner = jnp.concatenate([last[:, :half], last[:, half:]], axis=0)
    bottom = jnp.concatenate([jnp.zeros((half, half), F32), corner], axis=1)
    return jnp.concatenate([top, bottom], axis=0), w


def first_kernel(
    side, own_a, own_b, other_a, other_b, own_w, other_w, q_out, state, send
):
    q, upper, w = merge_math(
        (own_a[...] + own_b[...], (own_w[...],), None),
        (other_a[...] + other_b[...], (other_w[...],), None),
        1,
        True,
    )
    store_state(side, upper, w, state, send)
    q_out[...] = q


def upper_kernel(level, is_last, has_buffer, side, own, own_p, near, far, other_p, *refs):
    refs = list(refs)
    if has_buffer:
        refs.pop(0)
    q_all = refs.pop(0)
    outs = [] if is_last else [refs.pop(0), refs.pop(0)]
    q_here, done = refs
    is_first = side[0] == 0
    own_s, own_w = load_state(own[0], own[1])
    near, far = near[...], far[...]
    other_s, other_w = load_state(jnp.where(is_first, near, far), jnp.where(is_first, far, near))
    q, upper, w = merge_math(
        (own_s, split(own_w), split(own_p[...])),
        (other_s, split(other_w), split(other_p[...])),
        level,
        not is_last,
    )
    q_here[...] = q
    copy = pltpu.make_async_copy(q_here, q_all.at[level - 2], done)
    copy.start()
    if not is_last:
        store_state(side, upper, w, *outs)
    copy.wait()


VMEM = pl.BlockSpec(memory_space=pltpu.VMEM)
SMEM = pl.BlockSpec(memory_space=pltpu.SMEM)
ANY = pl.BlockSpec(memory_space=pl.ANY)


def near_core(arrays):
    return [pltpu.with_memory_space_constraint(x, pltpu.VMEM) for x in arrays]


def state_shapes(size):
    rows = size // 2 + 3 * size // 8
    return [pltpu.VMEM((2, rows, size), F32), pltpu.VMEM((rows, size), F32)]


def first_merge(side, arrays):
    rows, size = arrays[0].shape
    return pl.pallas_call(
        first_kernel,
        out_shape=[jax.ShapeDtypeStruct((rows, size), F32)] + state_shapes(size),
        in_specs=[SMEM] + [VMEM] * len(arrays),
        out_specs=[VMEM] * 3,
        compiler_params=pltpu.CompilerParams(vmem_limit_bytes=SCRATCH_BYTES),
        name="first_merge",
    )(side, *near_core(arrays))


def upper_merge(level, levels, side, arrays, buffer):
    size = arrays[1].shape[1]
    is_last = level == levels
    extra = [] if buffer is None else [buffer]
    out_shape = [jax.ShapeDtypeStruct((levels - 1, size, size), F32)]
    out_shape += [] if is_last else state_shapes(size)
    return pl.pallas_call(
        functools.partial(upper_kernel, level, is_last, bool(extra)),
        out_shape=out_shape,
        in_specs=[SMEM] + [VMEM] * len(arrays) + [ANY] * len(extra),
        out_specs=[ANY] + [VMEM] * (len(out_shape) - 1),
        scratch_shapes=[pltpu.VMEM((size, size), F32), pltpu.SemaphoreType.DMA(())],
        input_output_aliases={1 + len(arrays): 0} if extra else {},
        compiler_params=pltpu.CompilerParams(vmem_limit_bytes=SCRATCH_BYTES),
    )(side, *near_core(arrays), *extra)


def load_kernel(keys, place, mask, front, own, rows, own_here, arrived):
    slots, leaf = rows.shape[:2]
    own_copy = pltpu.make_async_copy(own, own_here, arrived.at[slots, 0])
    own_copy.start()
    tiles = []
    for slot in range(slots):
        for j, key in enumerate(keys):
            tile_row, chunk = place[1] ^ slot, place[0] ^ key
            row_tile = place[0] * slots + tile_row
            col_tile = place[1] * len(keys) + chunk
            present = (mask[tile_row, chunk] != 0) & (row_tile // 2 != col_tile // 2)
            here = rows.at[slot, :, pl.ds(j * leaf, leaf)]
            copy = pltpu.make_async_copy(
                front.at[
                    pl.ds(pl.multiple_of(tile_row * leaf, leaf), leaf),
                    pl.ds(pl.multiple_of(chunk * leaf, leaf), leaf),
                ],
                here,
                arrived.at[slot, j],
            )
            tiles.append((present, copy))

            @pl.when(present)
            def _():
                copy.start()

            @pl.when(jnp.logical_not(present))
            def _():
                here[...] = jnp.zeros(here.shape, BF16)

    for present, copy in tiles:

        @pl.when(present)
        def _():
            copy.wait()

    own_copy.wait()


def load_front(front, tile_mask, place, own, keys):
    leaf, size = own.shape
    slots, width = front.shape[0] // leaf, front.shape[1]
    small = width * size < 2**20
    form = pltpu.VMEM if small else jax.ShapeDtypeStruct
    return pl.pallas_call(
        functools.partial(load_kernel, keys),
        out_shape=[form((slots, leaf, width), BF16), form((leaf, size), BF16)],
        in_specs=[SMEM, SMEM, ANY, ANY],
        out_specs=[VMEM] * 2,
        scratch_shapes=[pltpu.SemaphoreType.DMA((slots + 1, len(keys)))],
        compiler_params=pltpu.CompilerParams(vmem_limit_bytes=SCRATCH_BYTES * (1 if small else 3)),
        name="load_front",
    )(
        place,
        tile_mask,
        pltpu.with_memory_space_constraint(front, pltpu.HBM),
        pltpu.with_memory_space_constraint(own, pltpu.HBM),
    )


def sample_kernel(rows, *refs):
    chunks, (keep, send) = refs[:-2], refs[-2:]
    slots = rows.shape[0]
    probes = jnp.concatenate([x[...] for x in chunks], axis=0)
    for slot in [*range(1, slots, 2), *range(0, slots, 2)]:
        out = send if slot % 2 else keep
        out[slot // 2] = dot(rows[slot], probes, (1, 0))


def all_samples(rows, chunks):
    slots, leaf, width = rows.shape
    size = chunks[0].shape[1]
    small = width * size < 2**20
    form = pltpu.VMEM if small else jax.ShapeDtypeStruct
    arrays = [rows, *chunks]
    return pl.pallas_call(
        sample_kernel,
        out_shape=[form((slots // 2, leaf, size), F32)] * 2,
        in_specs=[VMEM] * len(arrays),
        out_specs=[VMEM] * 2,
        compiler_params=pltpu.CompilerParams(vmem_limit_bytes=SCRATCH_BYTES * (1 if small else 3)),
        name="samples",
    )(*(near_core(arrays) if small else arrays))


def swap(x, axis, bit):
    return lax.ppermute(x, axis, [(i, i ^ (1 << bit)) for i in range(lax.axis_size(axis))])


def step(front, tile_mask, probes, coupling):
    col_count, row_count = lax.axis_size("col"), lax.axis_size("row")
    row_index, col_index = lax.axis_index("row"), lax.axis_index("col")
    col_levels, row_levels = col_count.bit_length() - 1, row_count.bit_length() - 1
    levels = col_levels + row_levels
    place = jnp.stack([row_index, col_index]).astype(jnp.int32)
    side = (col_index & 1).astype(jnp.int32)[None]
    bits = [("col", b) for b in range(col_levels)] + [("row", b) for b in range(row_levels)]

    chunks = {0: probes}
    chunks[1] = swap(probes, "row", 0)
    for bit in range(row_levels - 1, 0, -1):
        for key in list(chunks):
            new = key | 1 << bit
            if key == 1:
                chunks[new] = swap(chunks[new ^ 1], "row", 0)
            else:
                chunks[new] = swap(chunks[key], "row", bit)

    home = [((b % row_count) * col_count + b // row_count, b) for b in range(row_count * col_count)]
    own_w = lax.ppermute(probes, ("row", "col"), home)
    other_w = lax.ppermute(probes, ("row", "col"), [(at, b ^ 1) for at, b in home])

    own_p, other_p, total_p = {}, {}, coupling
    for level, (axis, bit) in enumerate(bits, start=1):
        own_p[level], other_p[level] = total_p, swap(total_p, axis, bit)
        if level < levels:
            total_p = own_p[level] + other_p[level]

    order = list(chunks)
    rows, own_chunk = load_front(front, tile_mask, place, probes, order)
    keep, send = all_samples(rows, [own_chunk] + [chunks[k] for k in order[1:]])
    got = swap(send, "col", 0)
    slots = {2 * k: (keep[k], got[k]) for k in range(col_count // 2)}
    for bit in range(1, col_levels):
        far = 1 << bit
        left = list(range(0, col_count, 2 * far))
        moved = swap(jnp.stack([slots[k + far][0] + slots[k + far][1] for k in left]), "col", bit)
        slots = {k: (slots[k][0] + slots[k][1], moved[i]) for i, k in enumerate(left)}
    own_a, own_b = slots[0]
    other_a = swap(own_a, "col", 0)
    other_b = swap(own_b, "col", 0)

    leaf_basis, state, send = first_merge(
        side, (own_a, own_b, other_a, other_b, own_w, other_w)
    )
    buffer = None
    for level, (axis, bit) in list(enumerate(bits, start=1))[1:]:
        near = swap(send, axis, bit)
        far = swap(near, "col", 0)
        buffer, *rest = upper_merge(
            level, levels, side, (state, own_p[level], near, far, other_p[level]), buffer
        )
        if rest:
            state, send = rest
    return (leaf_basis, buffer)


def solution(mesh):
    in_specs = (P("row", "col"), P("row", "col"), P(("col", "row"), None), P(("row", "col"), None))
    out_specs = (P(("row", "col"), None), P(None, ("row", "col"), None))
    return jax.shard_map(step, mesh=mesh, in_specs=in_specs, out_specs=out_specs, check_vma=False)
```

```python
import functools

import jax
import jax.numpy as jnp
from jax import lax
from jax.experimental import pallas as pl
from jax.experimental.pallas import tpu as pltpu
from jax.sharding import PartitionSpec as P

F32 = jnp.float32
BF16 = jnp.bfloat16
SUB, LANE = 8, 128
BLOCK = LANE // 2
PANEL = 2
SCRATCH_BYTES = 16 * 2**20


def split(x):
    high = x.astype(BF16)
    return high, (x - high.astype(F32)).astype(BF16)


def dot(left, right, dims):
    return lax.dot_general(
        left, right, (((dims[0],), (dims[1],)), ((), ())), preferred_element_type=F32
    )


def product(left, right, dims):
    total = None
    for i in reversed(range(len(left))):
        for j in reversed(range(len(right))):
            if i + j < 2:
                term = dot(left[i], right[j], dims)
                total = term if total is None else total + term
    return total


def lane_copy(x, lane):
    return jnp.take_along_axis(
        x, jnp.full(x.shape, lane, jnp.int32), axis=1, mode="promise_in_bounds"
    )


def row_copy(x, row):
    return jnp.broadcast_to(x[row : row + 1, :], x.shape)


def tree_sum(terms):
    while len(terms) > 1:
        pairs = [terms[i] + terms[i + 1] for i in range(0, len(terms) - 1, 2)]
        terms = pairs + terms[len(pairs) * 2 :]
    return terms[0]


def factor_block(packed, offset):
    count = BLOCK // SUB
    rows = [packed[SUB * k : SUB * (k + 1), :] for k in range(count)]
    sub = lax.broadcasted_iota(jnp.int32, (SUB, LANE), 0)
    out = []
    for first in range(0, count, PANEL):
        width, start = SUB * PANEL, offset + SUB * first
        held = rows[first : first + PANEL]
        cols = [[lane_copy(held[q], start + t) for q in range(PANEL)] for t in range(width)]
        done, scales = [None] * PANEL, [None] * PANEL
        for s in range(width):
            own, at = divmod(s, SUB)
            if at == 0:
                for t in range(s, width):
                    for q in range(own):
                        cols[t][q] = lane_copy(held[q], start + t)
            here = sub == at
            pivot = row_copy(cols[s][own], at)
            scale = 1.0 / pivot
            root = lax.rsqrt(pivot)
            bare = [jnp.where(here, 0.0, cols[s][q]) if q == own else cols[s][q] for q in range(PANEL)]
            factor = [x * scale for x in bare]
            row = row_copy(held[own], at)
            if at == 0:
                done[own], scales[own] = row * root, scale
            else:
                done[own] = jnp.where(here, row * root, done[own])
                scales[own] = jnp.where(here, scale, scales[own])
            for t in range(s + 1, width):
                across = row_copy(cols[s][t // SUB], t % SUB)
                for q in range(PANEL):
                    if q < t // SUB and own < t // SUB:
                        continue
                    if t == s + 1:
                        cols[t][q] = cols[t][q] - (bare[q] * across) * scale
                    else:
                        cols[t][q] = cols[t][q] - factor[q] * across
            for q in range(PANEL):
                held[q] = held[q] - factor[q] * row
        out += done
        if first + PANEL < count:
            held = [held[q] * scales[q] for q in range(PANEL)]
            solved = [row_copy(held[s // SUB], s % SUB) for s in range(width)]
            for k in range(first + PANEL, count):
                weight = [lane_copy(rows[k], start + s) for s in range(width)]
                rows[k] = rows[k] - tree_sum([weight[s] * solved[s] for s in range(width)])
    return jnp.concatenate(out, axis=0)


def four(x):
    high, low = split(x)
    return jnp.concatenate([high, high, low, low], axis=0)


def two_parts(x):
    high = x.astype(BF16).astype(F32)
    return high, x - high


def factor_all(gram, rights):
    count = gram.shape[0] // BLOCK
    lane = lax.broadcasted_iota(jnp.int32, (BLOCK, LANE), 1)
    sub = lax.broadcasted_iota(jnp.int32, (BLOCK, LANE), 0)
    blocks = [gram[BLOCK * i : BLOCK * (i + 1), :] for i in range(count)]
    rights = [[x[BLOCK * i : BLOCK * (i + 1), :] for i in range(count)] for x in rights]
    upper, solved = [], [[] for _ in rights]
    for i in range(count):
        first, offset = BLOCK * i // LANE * LANE, BLOCK * i % LANE
        other = BLOCK - offset
        mine = (lane >= offset) & (lane < offset + BLOCK)
        tile = slice(first, first + LANE)
        both = factor_block(
            jnp.where(mine, blocks[i][:, tile], jnp.where(lane - other == sub, 1.0, 0.0)), offset
        )
        high, low = two_parts(jnp.where(mine, 0.0, both))
        low_here = pltpu.roll(low, BLOCK, 1)
        left = jnp.concatenate([jnp.where(mine, low_here, high), high], axis=1).astype(BF16)
        row = both
        if i + 1 < count:
            row = dot(left, four(blocks[i][:, first:]), (1, 0))
            high_here = pltpu.roll(high, BLOCK, 1)
            across = jnp.concatenate([high_here, low_here, high_here], axis=1).astype(BF16)
            below = jnp.concatenate([blocks[j][:, tile] for j in range(i + 1, count)], axis=0)
            high, low = split(below)
            column = dot(
                jnp.concatenate([high, high, low], axis=1),
                jnp.concatenate([across, across], axis=0),
                (1, 1),
            )
            high, low = two_parts(column)
            near = lax.broadcasted_iota(jnp.int32, column.shape, 1) < BLOCK
            column = jnp.concatenate(
                [jnp.where(near, high, low), jnp.where(near, high, 0.0)], axis=1
            ).astype(BF16)
            change = dot(column, four(row), (1, 0))
            for j in range(i + 1, count):
                at = BLOCK * (j - i - 1)
                new = blocks[j][:, first:] - change[at : at + BLOCK, :]
                if first:
                    new = jnp.concatenate([blocks[j][:, :first], new], axis=1)
                blocks[j] = new
        for x, y in zip(rights, solved):
            y.append(dot(left, four(x[i]), (1, 0)))
            if i + 1 < count:
                change = dot(column, four(y[i]), (1, 0))
                for j in range(i + 1, count):
                    at = BLOCK * (j - i - 1)
                    x[j] = x[j] - change[at : at + BLOCK, :]
        head = jnp.where(mine, both, row[:, :LANE])
        head = jnp.where(lane < offset + jnp.where(mine, sub, 0), 0.0, head)
        upper.append(head if row.shape[1] == LANE else jnp.concatenate([head, row[:, LANE:]], axis=1))
    return upper, [jnp.concatenate(x, axis=0) for x in solved]


def merge_math(own, other, level, want_state):
    own_s, own_w, own_p = own
    other_s, other_w, other_p = other
    if level > 1:
        factor = 2.0 ** (-(level - 1) / 2.0)
        own_s = own_s - factor * product(own_p, other_w, (1, 0))
        other_s = other_s - factor * product(other_p, own_w, (1, 0))
    size = own_s.shape[1]
    own_h, other_h = split(own_s), split(other_s)
    gram = product(own_h, own_h, (0, 0)) + product(other_h, other_h, (0, 0))
    trace = jnp.sum(own_s * own_s) + jnp.sum(other_s * other_s)
    shift = 0.001 * (trace / size + 1e-06)
    eye = lax.broadcasted_iota(jnp.int32, (size, size), 0) == lax.broadcasted_iota(
        jnp.int32, (size, size), 1
    )
    rights = [jnp.where(eye, 1.0, 0.0)]
    if want_state:
        rights.append(product(own_h, own_w, (0, 0)) + product(other_h, other_w, (0, 0)))
    upper, solved = factor_all(gram + jnp.where(eye, shift, 0.0), rights)
    q = product(own_h, split(solved[0]), (1, 1))
    return q, upper, solved[1] if want_state else None


def store_state(side, upper, w, state, send):
    half = w.shape[0] // 2
    part = half // 2
    share = half - part // 2
    state[0, :half] = w[:half]
    state[1, :half] = w[half:]
    top = jnp.concatenate(upper[:2], axis=0)
    state[0, half:] = top[:share]
    state[1, half : half + half - share] = top[share:]
    state[1, half + half - share :] = jnp.concatenate(upper[2:], axis=1)
    send[...] = state[side[0]]


def load_state(first, second):
    half = first.shape[1] // 2
    part = half // 2
    share = half - part // 2
    w = jnp.concatenate([first[:half], second[:half]], axis=0)
    split_at = half + half - share
    top = jnp.concatenate([first[half:], second[half:split_at]], axis=0)
    last = second[split_at:]
    corner = jnp.concatenate([last[:, :half], last[:, half:]], axis=0)
    bottom = jnp.concatenate([jnp.zeros((half, half), F32), corner], axis=1)
    return jnp.concatenate([top, bottom], axis=0), w


def first_kernel(
    side, own_a, own_b, other_a, other_b, own_w, other_w, q_out, state, send
):
    q, upper, w = merge_math(
        (own_a[...] + own_b[...], (own_w[...],), None),
        (other_a[...] + other_b[...], (other_w[...],), None),
        1,
        True,
    )
    store_state(side, upper, w, state, send)
    q_out[...] = q


def upper_kernel(level, is_last, has_buffer, side, own, own_p, near, far, other_p, *refs):
    refs = list(refs)
    if has_buffer:
        refs.pop(0)
    q_all = refs.pop(0)
    outs = [] if is_last else [refs.pop(0), refs.pop(0)]
    q_here, done = refs
    is_first = side[0] == 0
    own_s, own_w = load_state(own[0], own[1])
    near, far = near[...], far[...]
    other_s, other_w = load_state(jnp.where(is_first, near, far), jnp.where(is_first, far, near))
    q, upper, w = merge_math(
        (own_s, split(own_w), split(own_p[...])),
        (other_s, split(other_w), split(other_p[...])),
        level,
        not is_last,
    )
    q_here[...] = q
    copy = pltpu.make_async_copy(q_here, q_all.at[level - 2], done)
    copy.start()
    if not is_last:
        store_state(side, upper, w, *outs)
    copy.wait()


VMEM = pl.BlockSpec(memory_space=pltpu.VMEM)
SMEM = pl.BlockSpec(memory_space=pltpu.SMEM)
ANY = pl.BlockSpec(memory_space=pl.ANY)


def near_core(arrays):
    return [pltpu.with_memory_space_constraint(x, pltpu.VMEM) for x in arrays]


def state_shapes(size):
    rows = size // 2 + 3 * size // 8
    return [pltpu.VMEM((2, rows, size), F32), pltpu.VMEM((rows, size), F32)]


def first_merge(side, arrays):
    rows, size = arrays[0].shape
    return pl.pallas_call(
        first_kernel,
        out_shape=[jax.ShapeDtypeStruct((rows, size), F32)] + state_shapes(size),
        in_specs=[SMEM] + [VMEM] * len(arrays),
        out_specs=[VMEM] * 3,
        compiler_params=pltpu.CompilerParams(vmem_limit_bytes=SCRATCH_BYTES),
        name="first_merge",
    )(side, *near_core(arrays))


def upper_merge(level, levels, side, arrays, buffer):
    size = arrays[1].shape[1]
    is_last = level == levels
    extra = [] if buffer is None else [buffer]
    out_shape = [jax.ShapeDtypeStruct((levels - 1, size, size), F32)]
    out_shape += [] if is_last else state_shapes(size)
    return pl.pallas_call(
        functools.partial(upper_kernel, level, is_last, bool(extra)),
        out_shape=out_shape,
        in_specs=[SMEM] + [VMEM] * len(arrays) + [ANY] * len(extra),
        out_specs=[ANY] + [VMEM] * (len(out_shape) - 1),
        scratch_shapes=[pltpu.VMEM((size, size), F32), pltpu.SemaphoreType.DMA(())],
        input_output_aliases={1 + len(arrays): 0} if extra else {},
        compiler_params=pltpu.CompilerParams(vmem_limit_bytes=SCRATCH_BYTES),
    )(side, *near_core(arrays), *extra)


def load_kernel(keys, place, mask, front, own, rows, own_here, arrived):
    slots, leaf = rows.shape[:2]
    own_copy = pltpu.make_async_copy(own, own_here, arrived.at[slots, 0])
    own_copy.start()
    tiles = []
    for slot in range(slots):
        for j, key in enumerate(keys):
            tile_row, chunk = place[1] ^ slot, place[0] ^ key
            row_tile = place[0] * slots + tile_row
            col_tile = place[1] * len(keys) + chunk
            present = (mask[tile_row, chunk] != 0) & (row_tile // 2 != col_tile // 2)
            here = rows.at[slot, :, pl.ds(j * leaf, leaf)]
            copy = pltpu.make_async_copy(
                front.at[
                    pl.ds(pl.multiple_of(tile_row * leaf, leaf), leaf),
                    pl.ds(pl.multiple_of(chunk * leaf, leaf), leaf),
                ],
                here,
                arrived.at[slot, j],
            )
            tiles.append((present, copy))

            @pl.when(present)
            def _():
                copy.start()

            @pl.when(jnp.logical_not(present))
            def _():
                here[...] = jnp.zeros(here.shape, BF16)

    for present, copy in tiles:

        @pl.when(present)
        def _():
            copy.wait()

    own_copy.wait()


def load_front(front, tile_mask, place, own, keys):
    leaf, size = own.shape
    slots, width = front.shape[0] // leaf, front.shape[1]
    small = width * size < 2**20
    form = pltpu.VMEM if small else jax.ShapeDtypeStruct
    return pl.pallas_call(
        functools.partial(load_kernel, keys),
        out_shape=[form((slots, leaf, width), BF16), form((leaf, size), BF16)],
        in_specs=[SMEM, SMEM, ANY, ANY],
        out_specs=[VMEM] * 2,
        scratch_shapes=[pltpu.SemaphoreType.DMA((slots + 1, len(keys)))],
        compiler_params=pltpu.CompilerParams(vmem_limit_bytes=SCRATCH_BYTES * (1 if small else 3)),
        name="load_front",
    )(
        place,
        tile_mask,
        pltpu.with_memory_space_constraint(front, pltpu.HBM),
        pltpu.with_memory_space_constraint(own, pltpu.HBM),
    )


def sample_kernel(rows, *refs):
    chunks, (keep, send) = refs[:-2], refs[-2:]
    slots = rows.shape[0]
    probes = jnp.concatenate([x[...] for x in chunks], axis=0)
    for slot in [*range(1, slots, 2), *range(0, slots, 2)]:
        out = send if slot % 2 else keep
        out[slot // 2] = dot(rows[slot], probes, (1, 0))


def all_samples(rows, chunks):
    slots, leaf, width = rows.shape
    size = chunks[0].shape[1]
    small = width * size < 2**20
    form = pltpu.VMEM if small else jax.ShapeDtypeStruct
    arrays = [rows, *chunks]
    return pl.pallas_call(
        sample_kernel,
        out_shape=[form((slots // 2, leaf, size), F32)] * 2,
        in_specs=[VMEM] * len(arrays),
        out_specs=[VMEM] * 2,
        compiler_params=pltpu.CompilerParams(vmem_limit_bytes=SCRATCH_BYTES * (1 if small else 3)),
        name="samples",
    )(*(near_core(arrays) if small else arrays))


def swap(x, axis, bit):
    return lax.ppermute(x, axis, [(i, i ^ (1 << bit)) for i in range(lax.axis_size(axis))])


def step(front, tile_mask, probes, coupling):
    col_count, row_count = lax.axis_size("col"), lax.axis_size("row")
    row_index, col_index = lax.axis_index("row"), lax.axis_index("col")
    col_levels, row_levels = col_count.bit_length() - 1, row_count.bit_length() - 1
    levels = col_levels + row_levels
    place = jnp.stack([row_index, col_index]).astype(jnp.int32)
    side = (col_index & 1).astype(jnp.int32)[None]
    bits = [("col", b) for b in range(col_levels)] + [("row", b) for b in range(row_levels)]

    chunks = {0: probes}
    chunks[1] = swap(probes, "row", 0)
    for bit in range(row_levels - 1, 0, -1):
        for key in list(chunks):
            new = key | 1 << bit
            if key == 1:
                chunks[new] = swap(chunks[new ^ 1], "row", 0)
            else:
                chunks[new] = swap(chunks[key], "row", bit)

    home = [((b % row_count) * col_count + b // row_count, b) for b in range(row_count * col_count)]
    own_w = lax.ppermute(probes, ("row", "col"), home)
    other_w = swap(own_w, "col", 0)

    own_p, other_p, total_p = {}, {}, coupling
    for level, (axis, bit) in enumerate(bits, start=1):
        own_p[level], other_p[level] = total_p, swap(total_p, axis, bit)
        if level < levels:
            total_p = own_p[level] + other_p[level]

    order = list(chunks)
    rows, own_chunk = load_front(front, tile_mask, place, probes, order)
    keep, send = all_samples(rows, [own_chunk] + [chunks[k] for k in order[1:]])
    got = swap(send, "col", 0)
    slots = {2 * k: (keep[k], got[k]) for k in range(col_count // 2)}
    for bit in range(1, col_levels):
        far = 1 << bit
        left = list(range(0, col_count, 2 * far))
        moved = swap(jnp.stack([slots[k + far][0] + slots[k + far][1] for k in left]), "col", bit)
        slots = {k: (slots[k][0] + slots[k][1], moved[i]) for i, k in enumerate(left)}
    own_a, own_b = slots[0]
    other_a = swap(own_a, "col", 0)
    other_b = swap(own_b, "col", 0)

    leaf_basis, state, send = first_merge(
        side, (own_a, own_b, other_a, other_b, own_w, other_w)
    )
    buffer = None
    for level, (axis, bit) in list(enumerate(bits, start=1))[1:]:
        near = swap(send, axis, bit)
        far = swap(near, "col", 0)
        buffer, *rest = upper_merge(
            level, levels, side, (state, own_p[level], near, far, other_p[level]), buffer
        )
        if rest:
            state, send = rest
    return (leaf_basis, buffer)


def solution(mesh):
    in_specs = (P("row", "col"), P("row", "col"), P(("col", "row"), None), P(("row", "col"), None))
    out_specs = (P(("row", "col"), None), P(None, ("row", "col"), None))
    return jax.shard_map(step, mesh=mesh, in_specs=in_specs, out_specs=out_specs, check_vma=False)
```

```python
import functools

import jax
import jax.numpy as jnp
from jax import lax
from jax.experimental import pallas as pl
from jax.experimental.pallas import tpu as pltpu
from jax.sharding import PartitionSpec as P

F32 = jnp.float32
BF16 = jnp.bfloat16
SUB, LANE = 8, 128
BLOCK = LANE // 2
PANEL = 2
SCRATCH_BYTES = 16 * 2**20


def split(x):
    high = x.astype(BF16)
    return high, (x - high.astype(F32)).astype(BF16)


def dot(left, right, dims):
    return lax.dot_general(
        left, right, (((dims[0],), (dims[1],)), ((), ())), preferred_element_type=F32
    )


def product(left, right, dims):
    total = None
    for i in reversed(range(len(left))):
        for j in reversed(range(len(right))):
            if i + j < 2:
                term = dot(left[i], right[j], dims)
                total = term if total is None else total + term
    return total


def lane_copy(x, lane):
    return jnp.take_along_axis(
        x, jnp.full(x.shape, lane, jnp.int32), axis=1, mode="promise_in_bounds"
    )


def row_copy(x, row):
    return jnp.broadcast_to(x[row : row + 1, :], x.shape)


def tree_sum(terms):
    while len(terms) > 1:
        pairs = [terms[i] + terms[i + 1] for i in range(0, len(terms) - 1, 2)]
        terms = pairs + terms[len(pairs) * 2 :]
    return terms[0]


def factor_block(packed, offset):
    count = BLOCK // SUB
    rows = [packed[SUB * k : SUB * (k + 1), :] for k in range(count)]
    sub = lax.broadcasted_iota(jnp.int32, (SUB, LANE), 0)
    out = []
    for first in range(0, count, PANEL):
        width, start = SUB * PANEL, offset + SUB * first
        held = rows[first : first + PANEL]
        cols = [[lane_copy(held[q], start + t) for q in range(PANEL)] for t in range(width)]
        done, scales = [None] * PANEL, [None] * PANEL
        for s in range(width):
            own, at = divmod(s, SUB)
            if at == 0:
                for t in range(s, width):
                    for q in range(own):
                        cols[t][q] = lane_copy(held[q], start + t)
            here = sub == at
            pivot = row_copy(cols[s][own], at)
            scale = 1.0 / pivot
            root = lax.rsqrt(pivot)
            bare = [jnp.where(here, 0.0, cols[s][q]) if q == own else cols[s][q] for q in range(PANEL)]
            factor = [x * scale for x in bare]
            row = row_copy(held[own], at)
            if at == 0:
                done[own], scales[own] = row * root, scale
            else:
                done[own] = jnp.where(here, row * root, done[own])
                scales[own] = jnp.where(here, scale, scales[own])
            for t in range(s + 1, width):
                across = row_copy(cols[s][t // SUB], t % SUB)
                for q in range(PANEL):
                    if q < t // SUB and own < t // SUB:
                        continue
                    if t == s + 1:
                        cols[t][q] = cols[t][q] - (bare[q] * across) * scale
                    else:
                        cols[t][q] = cols[t][q] - factor[q] * across
            for q in range(PANEL):
                held[q] = held[q] - factor[q] * row
        out += done
        if first + PANEL < count:
            held = [held[q] * scales[q] for q in range(PANEL)]
            solved = [row_copy(held[s // SUB], s % SUB) for s in range(width)]
            for k in range(first + PANEL, count):
                weight = [lane_copy(rows[k], start + s) for s in range(width)]
                rows[k] = rows[k] - tree_sum([weight[s] * solved[s] for s in range(width)])
    return jnp.concatenate(out, axis=0)


def four(x):
    high, low = split(x)
    return jnp.concatenate([high, high, low, low], axis=0)


def two_parts(x):
    high = x.astype(BF16).astype(F32)
    return high, x - high


def factor_all(gram, rights):
    count = gram.shape[0] // BLOCK
    lane = lax.broadcasted_iota(jnp.int32, (BLOCK, LANE), 1)
    sub = lax.broadcasted_iota(jnp.int32, (BLOCK, LANE), 0)
    blocks = [gram[BLOCK * i : BLOCK * (i + 1), :] for i in range(count)]
    rights = [[x[BLOCK * i : BLOCK * (i + 1), :] for i in range(count)] for x in rights]
    upper, solved = [], [[] for _ in rights]
    for i in range(count):
        first, offset = BLOCK * i // LANE * LANE, BLOCK * i % LANE
        other = BLOCK - offset
        mine = (lane >= offset) & (lane < offset + BLOCK)
        tile = slice(first, first + LANE)
        both = factor_block(
            jnp.where(mine, blocks[i][:, tile], jnp.where(lane - other == sub, 1.0, 0.0)), offset
        )
        high, low = two_parts(jnp.where(mine, 0.0, both))
        low_here = pltpu.roll(low, BLOCK, 1)
        left = jnp.concatenate([jnp.where(mine, low_here, high), high], axis=1).astype(BF16)
        row = both
        if i + 1 < count:
            row = dot(left, four(blocks[i][:, first:]), (1, 0))
            high_here = pltpu.roll(high, BLOCK, 1)
            across = jnp.concatenate([high_here, low_here, high_here], axis=1).astype(BF16)
            below = jnp.concatenate([blocks[j][:, tile] for j in range(i + 1, count)], axis=0)
            high, low = split(below)
            column = dot(
                jnp.concatenate([high, high, low], axis=1),
                jnp.concatenate([across, across], axis=0),
                (1, 1),
            )
            high, low = two_parts(column)
            near = lax.broadcasted_iota(jnp.int32, column.shape, 1) < BLOCK
            column = jnp.concatenate(
                [jnp.where(near, high, low), jnp.where(near, high, 0.0)], axis=1
            ).astype(BF16)
            change = dot(column, four(row), (1, 0))
            for j in range(i + 1, count):
                at = BLOCK * (j - i - 1)
                new = blocks[j][:, first:] - change[at : at + BLOCK, :]
                if first:
                    new = jnp.concatenate([blocks[j][:, :first], new], axis=1)
                blocks[j] = new
        for x, y in zip(rights, solved):
            y.append(dot(left, four(x[i]), (1, 0)))
            if i + 1 < count:
                change = dot(column, four(y[i]), (1, 0))
                for j in range(i + 1, count):
                    at = BLOCK * (j - i - 1)
                    x[j] = x[j] - change[at : at + BLOCK, :]
        head = jnp.where(mine, both, row[:, :LANE])
        head = jnp.where(lane < offset + jnp.where(mine, sub, 0), 0.0, head)
        upper.append(head if row.shape[1] == LANE else jnp.concatenate([head, row[:, LANE:]], axis=1))
    return upper, [jnp.concatenate(x, axis=0) for x in solved]


def merge_math(own, other, level, want_state):
    own_s, own_w, own_p = own
    other_s, other_w, other_p = other
    if level > 1:
        factor = 2.0 ** (-(level - 1) / 2.0)
        own_s = own_s - factor * product(own_p, other_w, (1, 0))
        other_s = other_s - factor * product(other_p, own_w, (1, 0))
    size = own_s.shape[1]
    own_h, other_h = split(own_s), split(other_s)
    gram = product(own_h, own_h, (0, 0)) + product(other_h, other_h, (0, 0))
    trace = jnp.sum(own_s * own_s) + jnp.sum(other_s * other_s)
    shift = 0.001 * (trace / size + 1e-06)
    eye = lax.broadcasted_iota(jnp.int32, (size, size), 0) == lax.broadcasted_iota(
        jnp.int32, (size, size), 1
    )
    rights = [jnp.where(eye, 1.0, 0.0)]
    if want_state:
        rights.append(product(own_h, own_w, (0, 0)) + product(other_h, other_w, (0, 0)))
    upper, solved = factor_all(gram + jnp.where(eye, shift, 0.0), rights)
    q = product(own_h, split(solved[0]), (1, 1))
    return q, upper, solved[1] if want_state else None


def store_state(side, upper, w, state, send):
    half = w.shape[0] // 2
    part = half // 2
    share = half - part // 2
    state[0, :half] = w[:half]
    state[1, :half] = w[half:]
    top = jnp.concatenate(upper[:2], axis=0)
    state[0, half:] = top[:share]
    state[1, half : half + half - share] = top[share:]
    state[1, half + half - share :] = jnp.concatenate(upper[2:], axis=1)
    rows = send.shape[0]
    if rows == state.shape[1]:
        send[...] = state[side[0]]
    else:
        send[...] = state[side[0], pl.ds(pl.multiple_of(side[1] * rows, SUB), rows)]


def load_state(first, second):
    half = first.shape[1] // 2
    part = half // 2
    share = half - part // 2
    w = jnp.concatenate([first[:half], second[:half]], axis=0)
    split_at = half + half - share
    top = jnp.concatenate([first[half:], second[half:split_at]], axis=0)
    last = second[split_at:]
    corner = jnp.concatenate([last[:, :half], last[:, half:]], axis=0)
    bottom = jnp.concatenate([jnp.zeros((half, half), F32), corner], axis=1)
    return jnp.concatenate([top, bottom], axis=0), w


def first_kernel(
    side, own_a, own_b, other_a, other_b, own_w, other_w, q_out, state, send
):
    q, upper, w = merge_math(
        (own_a[...] + own_b[...], (own_w[...],), None),
        (other_a[...] + other_b[...], (other_w[...],), None),
        1,
        True,
    )
    store_state(side, upper, w, state, send)
    q_out[...] = q


def gather_half(side, pieces):
    if len(pieces) == 1:
        return pieces[0][...]
    mine, theirs = pieces[0][...], pieces[1][...]
    is_first = side[1] == 0
    return jnp.concatenate(
        [jnp.where(is_first, mine, theirs), jnp.where(is_first, theirs, mine)], axis=0
    )


def upper_kernel(level, is_last, has_buffer, pieces, side, own, own_p, other_p, *refs):
    near, far, refs = list(refs[:pieces]), list(refs[pieces : 2 * pieces]), list(refs[2 * pieces :])
    if has_buffer:
        refs.pop(0)
    q_all = refs.pop(0)
    outs = [] if is_last else [refs.pop(0), refs.pop(0)]
    q_here, done = refs
    is_first = side[0] == 0
    own_s, own_w = load_state(own[0], own[1])
    near, far = gather_half(side, near), gather_half(side, far)
    other_s, other_w = load_state(jnp.where(is_first, near, far), jnp.where(is_first, far, near))
    q, upper, w = merge_math(
        (own_s, split(own_w), split(own_p[...])),
        (other_s, split(other_w), split(other_p[...])),
        level,
        not is_last,
    )
    q_here[...] = q
    copy = pltpu.make_async_copy(q_here, q_all.at[level - 2], done)
    copy.start()
    if not is_last:
        store_state(side, upper, w, *outs)
    copy.wait()


VMEM = pl.BlockSpec(memory_space=pltpu.VMEM)
SMEM = pl.BlockSpec(memory_space=pltpu.SMEM)
ANY = pl.BlockSpec(memory_space=pl.ANY)


def near_core(arrays):
    return [pltpu.with_memory_space_constraint(x, pltpu.VMEM) for x in arrays]


def state_shapes(size, pieces):
    rows = size // 2 + 3 * size // 8
    return [pltpu.VMEM((2, rows, size), F32), pltpu.VMEM((rows // pieces, size), F32)]


def first_merge(side, arrays, pieces):
    rows, size = arrays[0].shape
    return pl.pallas_call(
        first_kernel,
        out_shape=[jax.ShapeDtypeStruct((rows, size), F32)] + state_shapes(size, pieces),
        in_specs=[SMEM] + [VMEM] * len(arrays),
        out_specs=[VMEM] * 3,
        compiler_params=pltpu.CompilerParams(vmem_limit_bytes=SCRATCH_BYTES),
        name="first_merge",
    )(side, *near_core(arrays))


def upper_merge(level, levels, side, arrays, buffer, pieces):
    size = arrays[1].shape[1]
    is_last = level == levels
    extra = [] if buffer is None else [buffer]
    out_shape = [jax.ShapeDtypeStruct((levels - 1, size, size), F32)]
    out_shape += [] if is_last else state_shapes(size, pieces)
    return pl.pallas_call(
        functools.partial(upper_kernel, level, is_last, bool(extra), (len(arrays) - 3) // 2),
        out_shape=out_shape,
        in_specs=[SMEM] + [VMEM] * len(arrays) + [ANY] * len(extra),
        out_specs=[ANY] + [VMEM] * (len(out_shape) - 1),
        scratch_shapes=[pltpu.VMEM((size, size), F32), pltpu.SemaphoreType.DMA(())],
        input_output_aliases={1 + len(arrays): 0} if extra else {},
        compiler_params=pltpu.CompilerParams(vmem_limit_bytes=SCRATCH_BYTES),
    )(side, *near_core(arrays), *extra)


def load_kernel(keys, place, mask, front, own, rows, own_here, arrived):
    slots, leaf = rows.shape[:2]
    own_copy = pltpu.make_async_copy(own, own_here, arrived.at[slots, 0])
    own_copy.start()
    tiles = []
    for slot in range(slots):
        for j, key in enumerate(keys):
            tile_row, chunk = place[1] ^ slot, place[0] ^ key
            row_tile = place[0] * slots + tile_row
            col_tile = place[1] * len(keys) + chunk
            present = (mask[tile_row, chunk] != 0) & (row_tile // 2 != col_tile // 2)
            here = rows.at[slot, :, pl.ds(j * leaf, leaf)]
            copy = pltpu.make_async_copy(
                front.at[
                    pl.ds(pl.multiple_of(tile_row * leaf, leaf), leaf),
                    pl.ds(pl.multiple_of(chunk * leaf, leaf), leaf),
                ],
                here,
                arrived.at[slot, j],
            )
            tiles.append((present, copy))

            @pl.when(present)
            def _():
                copy.start()

            @pl.when(jnp.logical_not(present))
            def _():
                here[...] = jnp.zeros(here.shape, BF16)

    for present, copy in tiles:

        @pl.when(present)
        def _():
            copy.wait()

    own_copy.wait()


def load_front(front, tile_mask, place, own, keys):
    leaf, size = own.shape
    slots, width = front.shape[0] // leaf, front.shape[1]
    small = width * size < 2**20
    form = pltpu.VMEM if small else jax.ShapeDtypeStruct
    return pl.pallas_call(
        functools.partial(load_kernel, keys),
        out_shape=[form((slots, leaf, width), BF16), form((leaf, size), BF16)],
        in_specs=[SMEM, SMEM, ANY, ANY],
        out_specs=[VMEM] * 2,
        scratch_shapes=[pltpu.SemaphoreType.DMA((slots + 1, len(keys)))],
        compiler_params=pltpu.CompilerParams(vmem_limit_bytes=SCRATCH_BYTES * (1 if small else 3)),
        name="load_front",
    )(
        place,
        tile_mask,
        pltpu.with_memory_space_constraint(front, pltpu.HBM),
        pltpu.with_memory_space_constraint(own, pltpu.HBM),
    )


def sample_kernel(rows, *refs):
    chunks, (keep, send) = refs[:-2], refs[-2:]
    slots = rows.shape[0]
    probes = jnp.concatenate([x[...] for x in chunks], axis=0)
    for slot in [*range(1, slots, 2), *range(0, slots, 2)]:
        out = send if slot % 2 else keep
        out[slot // 2] = dot(rows[slot], probes, (1, 0))


def all_samples(rows, chunks):
    slots, leaf, width = rows.shape
    size = chunks[0].shape[1]
    small = width * size < 2**20
    form = pltpu.VMEM if small else jax.ShapeDtypeStruct
    arrays = [rows, *chunks]
    return pl.pallas_call(
        sample_kernel,
        out_shape=[form((slots // 2, leaf, size), F32)] * 2,
        in_specs=[VMEM] * len(arrays),
        out_specs=[VMEM] * 2,
        compiler_params=pltpu.CompilerParams(vmem_limit_bytes=SCRATCH_BYTES * (1 if small else 3)),
        name="samples",
    )(*(near_core(arrays) if small else arrays))


def swap(x, axis, bit):
    return lax.ppermute(x, axis, [(i, i ^ (1 << bit)) for i in range(lax.axis_size(axis))])


def step(front, tile_mask, probes, coupling):
    col_count, row_count = lax.axis_size("col"), lax.axis_size("row")
    row_index, col_index = lax.axis_index("row"), lax.axis_index("col")
    col_levels, row_levels = col_count.bit_length() - 1, row_count.bit_length() - 1
    levels = col_levels + row_levels
    place = jnp.stack([row_index, col_index]).astype(jnp.int32)
    side = jnp.stack([col_index & 1, col_index >> 1 & 1]).astype(jnp.int32)
    bits = [("col", b) for b in range(col_levels)] + [("row", b) for b in range(row_levels)]

    chunks = {0: probes}
    chunks[1] = swap(probes, "row", 0)
    for bit in range(row_levels - 1, 0, -1):
        for key in list(chunks):
            new = key | 1 << bit
            if key == 1:
                chunks[new] = swap(chunks[new ^ 1], "row", 0)
            else:
                chunks[new] = swap(chunks[key], "row", bit)

    home = [((b % row_count) * col_count + b // row_count, b) for b in range(row_count * col_count)]
    own_w = lax.ppermute(probes, ("row", "col"), home)
    other_w = swap(own_w, "col", 0)

    own_p, other_p, total_p = {}, {}, coupling
    for level, (axis, bit) in enumerate(bits, start=1):
        own_p[level], other_p[level] = total_p, swap(total_p, axis, bit)
        if level < levels:
            total_p = own_p[level] + other_p[level]

    order = list(chunks)
    rows, own_chunk = load_front(front, tile_mask, place, probes, order)
    keep, send = all_samples(rows, [own_chunk] + [chunks[k] for k in order[1:]])
    got = swap(send, "col", 0)
    slots = {2 * k: (keep[k], got[k]) for k in range(col_count // 2)}
    for bit in range(1, col_levels):
        far = 1 << bit
        left = list(range(0, col_count, 2 * far))
        moved = swap(jnp.stack([slots[k + far][0] + slots[k + far][1] for k in left]), "col", bit)
        slots = {k: (slots[k][0] + slots[k][1], moved[i]) for i, k in enumerate(left)}
    own_a, own_b = slots[0]
    other_a = swap(own_a, "col", 0)
    other_b = swap(own_b, "col", 0)

    def pieces(level):
        return 2 if level == levels and col_levels > 1 and row_levels > 0 else 1

    leaf_basis, state, send = first_merge(
        side, (own_a, own_b, other_a, other_b, own_w, other_w), pieces(2)
    )
    buffer = None
    for level, (axis, bit) in list(enumerate(bits, start=1))[1:]:
        near = [swap(send, axis, bit)]
        if pieces(level) > 1:
            near.append(swap(near[0], "col", 1))
        far = []
        for x in near:
            far.append(swap(x, "col", 0))
        buffer, *rest = upper_merge(
            level,
            levels,
            side,
            (state, own_p[level], other_p[level], *near, *far),
            buffer,
            pieces(level + 1),
        )
        if rest:
            state, send = rest
    return (leaf_basis, buffer)


def solution(mesh):
    in_specs = (P("row", "col"), P("row", "col"), P(("col", "row"), None), P(("row", "col"), None))
    out_specs = (P(("row", "col"), None), P(None, ("row", "col"), None))
    return jax.shard_map(step, mesh=mesh, in_specs=in_specs, out_specs=out_specs, check_vma=False)
```

```python
import functools

import jax
import jax.numpy as jnp
from jax import lax
from jax.experimental import pallas as pl
from jax.experimental.pallas import tpu as pltpu
from jax.sharding import PartitionSpec as P

F32 = jnp.float32
BF16 = jnp.bfloat16
SUB, LANE = 8, 128
BLOCK = LANE // 2
PANEL = 2
SCRATCH_BYTES = 16 * 2**20


def split(x):
    high = x.astype(BF16)
    return high, (x - high.astype(F32)).astype(BF16)


def dot(left, right, dims):
    return lax.dot_general(
        left, right, (((dims[0],), (dims[1],)), ((), ())), preferred_element_type=F32
    )


def product(left, right, dims):
    total = None
    for i in reversed(range(len(left))):
        for j in reversed(range(len(right))):
            if i + j < 2:
                term = dot(left[i], right[j], dims)
                total = term if total is None else total + term
    return total


def lane_copy(x, lane):
    return jnp.take_along_axis(
        x, jnp.full(x.shape, lane, jnp.int32), axis=1, mode="promise_in_bounds"
    )


def row_copy(x, row):
    return jnp.broadcast_to(x[row : row + 1, :], x.shape)


def tree_sum(terms):
    while len(terms) > 1:
        pairs = [terms[i] + terms[i + 1] for i in range(0, len(terms) - 1, 2)]
        terms = pairs + terms[len(pairs) * 2 :]
    return terms[0]


def factor_block(packed, offset):
    count = BLOCK // SUB
    rows = [packed[SUB * k : SUB * (k + 1), :] for k in range(count)]
    sub = lax.broadcasted_iota(jnp.int32, (SUB, LANE), 0)
    out = []
    for first in range(0, count, PANEL):
        width, start = SUB * PANEL, offset + SUB * first
        held = rows[first : first + PANEL]
        cols = [[lane_copy(held[q], start + t) for q in range(PANEL)] for t in range(width)]
        done, scales = [None] * PANEL, [None] * PANEL
        for s in range(width):
            own, at = divmod(s, SUB)
            if at == 0:
                for t in range(s, width):
                    for q in range(own):
                        cols[t][q] = lane_copy(held[q], start + t)
            here = sub == at
            pivot = row_copy(cols[s][own], at)
            scale = 1.0 / pivot
            root = lax.rsqrt(pivot)
            bare = [jnp.where(here, 0.0, cols[s][q]) if q == own else cols[s][q] for q in range(PANEL)]
            factor = [x * scale for x in bare]
            row = row_copy(held[own], at)
            if at == 0:
                done[own], scales[own] = row * root, scale
            else:
                done[own] = jnp.where(here, row * root, done[own])
                scales[own] = jnp.where(here, scale, scales[own])
            for t in range(s + 1, width):
                across = row_copy(cols[s][t // SUB], t % SUB)
                for q in range(PANEL):
                    if q < t // SUB and own < t // SUB:
                        continue
                    if t == s + 1:
                        cols[t][q] = cols[t][q] - (bare[q] * across) * scale
                    else:
                        cols[t][q] = cols[t][q] - factor[q] * across
            for q in range(PANEL):
                held[q] = held[q] - factor[q] * row
        out += done
        if first + PANEL < count:
            held = [held[q] * scales[q] for q in range(PANEL)]
            solved = [row_copy(held[s // SUB], s % SUB) for s in range(width)]
            for k in range(first + PANEL, count):
                weight = [lane_copy(rows[k], start + s) for s in range(width)]
                rows[k] = rows[k] - tree_sum([weight[s] * solved[s] for s in range(width)])
    return jnp.concatenate(out, axis=0)


def four(x):
    high, low = split(x)
    return jnp.concatenate([high, high, low, low], axis=0)


def two_parts(x):
    high = x.astype(BF16).astype(F32)
    return high, x - high


def factor_all(gram, rights):
    count = gram.shape[0] // BLOCK
    lane = lax.broadcasted_iota(jnp.int32, (BLOCK, LANE), 1)
    sub = lax.broadcasted_iota(jnp.int32, (BLOCK, LANE), 0)
    blocks = [gram[BLOCK * i : BLOCK * (i + 1), :] for i in range(count)]
    rights = [[x[BLOCK * i : BLOCK * (i + 1), :] for i in range(count)] for x in rights]
    upper, solved = [], [[] for _ in rights]
    for i in range(count):
        first, offset = BLOCK * i // LANE * LANE, BLOCK * i % LANE
        other = BLOCK - offset
        mine = (lane >= offset) & (lane < offset + BLOCK)
        tile = slice(first, first + LANE)
        both = factor_block(
            jnp.where(mine, blocks[i][:, tile], jnp.where(lane - other == sub, 1.0, 0.0)), offset
        )
        high, low = two_parts(jnp.where(mine, 0.0, both))
        low_here = pltpu.roll(low, BLOCK, 1)
        left = jnp.concatenate([jnp.where(mine, low_here, high), high], axis=1).astype(BF16)
        row = both
        if i + 1 < count:
            row = dot(left, four(blocks[i][:, first:]), (1, 0))
            high_here = pltpu.roll(high, BLOCK, 1)
            across = jnp.concatenate([high_here, low_here, high_here], axis=1).astype(BF16)
            below = jnp.concatenate([blocks[j][:, tile] for j in range(i + 1, count)], axis=0)
            high, low = split(below)
            column = dot(
                jnp.concatenate([high, high, low], axis=1),
                jnp.concatenate([across, across], axis=0),
                (1, 1),
            )
            high, low = two_parts(column)
            near = lax.broadcasted_iota(jnp.int32, column.shape, 1) < BLOCK
            column = jnp.concatenate(
                [jnp.where(near, high, low), jnp.where(near, high, 0.0)], axis=1
            ).astype(BF16)
            change = dot(column, four(row), (1, 0))
            for j in range(i + 1, count):
                at = BLOCK * (j - i - 1)
                new = blocks[j][:, first:] - change[at : at + BLOCK, :]
                if first:
                    new = jnp.concatenate([blocks[j][:, :first], new], axis=1)
                blocks[j] = new
        for x, y in zip(rights, solved):
            y.append(dot(left, four(x[i]), (1, 0)))
            if i + 1 < count:
                change = dot(column, four(y[i]), (1, 0))
                for j in range(i + 1, count):
                    at = BLOCK * (j - i - 1)
                    x[j] = x[j] - change[at : at + BLOCK, :]
        head = jnp.where(mine, both, row[:, :LANE])
        head = jnp.where(lane < offset + jnp.where(mine, sub, 0), 0.0, head)
        upper.append(head if row.shape[1] == LANE else jnp.concatenate([head, row[:, LANE:]], axis=1))
    return upper, [jnp.concatenate(x, axis=0) for x in solved]


def merge_math(own, other, level, want_state):
    own_s, own_w, own_p = own
    other_s, other_w, other_p = other
    if level > 1:
        factor = 2.0 ** (-(level - 1) / 2.0)
        own_s = own_s - factor * product(own_p, other_w, (1, 0))
        other_s = other_s - factor * product(other_p, own_w, (1, 0))
    size = own_s.shape[1]
    own_h, other_h = split(own_s), split(other_s)
    gram = product(own_h, own_h, (0, 0)) + product(other_h, other_h, (0, 0))
    trace = jnp.sum(own_s * own_s) + jnp.sum(other_s * other_s)
    shift = 0.001 * (trace / size + 1e-06)
    eye = lax.broadcasted_iota(jnp.int32, (size, size), 0) == lax.broadcasted_iota(
        jnp.int32, (size, size), 1
    )
    rights = [jnp.where(eye, 1.0, 0.0)]
    if want_state:
        rights.append(product(own_h, own_w, (0, 0)) + product(other_h, other_w, (0, 0)))
    upper, solved = factor_all(gram + jnp.where(eye, shift, 0.0), rights)
    q = product(own_h, split(solved[0]), (1, 1))
    return q, upper, solved[1] if want_state else None


def store_state(side, upper, w, state, send):
    half = w.shape[0] // 2
    part = half // 2
    share = half - part // 2
    state[0, :half] = w[:half]
    state[1, :half] = w[half:]
    top = jnp.concatenate(upper[:2], axis=0)
    state[0, half:] = top[:share]
    state[1, half : half + half - share] = top[share:]
    state[1, half + half - share :] = jnp.concatenate(upper[2:], axis=1)
    rows = send.shape[0]
    if rows == state.shape[1]:
        send[...] = state[side[0]]
    else:
        send[...] = state[side[0], pl.ds(pl.multiple_of(side[1] * rows, SUB), rows)]


def load_state(first, second):
    half = first.shape[1] // 2
    part = half // 2
    share = half - part // 2
    w = jnp.concatenate([first[:half], second[:half]], axis=0)
    split_at = half + half - share
    top = jnp.concatenate([first[half:], second[half:split_at]], axis=0)
    last = second[split_at:]
    corner = jnp.concatenate([last[:, :half], last[:, half:]], axis=0)
    bottom = jnp.concatenate([jnp.zeros((half, half), F32), corner], axis=1)
    return jnp.concatenate([top, bottom], axis=0), w


def chip_side():
    col = lax.axis_index("col")
    return col & 1, col >> 1 & 1


def first_kernel(
    own_a, own_b, other_a, other_b, own_w, other_w, q_out, state, send
):
    q, upper, w = merge_math(
        (own_a[...] + own_b[...], (own_w[...],), None),
        (other_a[...] + other_b[...], (other_w[...],), None),
        1,
        True,
    )
    store_state(chip_side(), upper, w, state, send)
    q_out[...] = q


def gather_half(side, pieces):
    if len(pieces) == 1:
        return pieces[0][...]
    mine, theirs = pieces[0][...], pieces[1][...]
    is_first = side[1] == 0
    return jnp.concatenate(
        [jnp.where(is_first, mine, theirs), jnp.where(is_first, theirs, mine)], axis=0
    )


def upper_kernel(level, is_last, has_buffer, pieces, own, own_p, other_p, *refs):
    side = chip_side()
    near, far, refs = list(refs[:pieces]), list(refs[pieces : 2 * pieces]), list(refs[2 * pieces :])
    if has_buffer:
        refs.pop(0)
    q_all = refs.pop(0)
    outs = [] if is_last else [refs.pop(0), refs.pop(0)]
    q_here, done = refs
    is_first = side[0] == 0
    own_s, own_w = load_state(own[0], own[1])
    near, far = gather_half(side, near), gather_half(side, far)
    other_s, other_w = load_state(jnp.where(is_first, near, far), jnp.where(is_first, far, near))
    q, upper, w = merge_math(
        (own_s, split(own_w), split(own_p[...])),
        (other_s, split(other_w), split(other_p[...])),
        level,
        not is_last,
    )
    q_here[...] = q
    copy = pltpu.make_async_copy(q_here, q_all.at[level - 2], done)
    copy.start()
    if not is_last:
        store_state(side, upper, w, *outs)
    copy.wait()


VMEM = pl.BlockSpec(memory_space=pltpu.VMEM)
SMEM = pl.BlockSpec(memory_space=pltpu.SMEM)
ANY = pl.BlockSpec(memory_space=pl.ANY)


def near_core(arrays):
    return [pltpu.with_memory_space_constraint(x, pltpu.VMEM) for x in arrays]


def state_shapes(size, pieces):
    rows = size // 2 + 3 * size // 8
    return [pltpu.VMEM((2, rows, size), F32), pltpu.VMEM((rows // pieces, size), F32)]


def first_merge(arrays, pieces):
    rows, size = arrays[0].shape
    return pl.pallas_call(
        first_kernel,
        out_shape=[jax.ShapeDtypeStruct((rows, size), F32)] + state_shapes(size, pieces),
        in_specs=[VMEM] * len(arrays),
        out_specs=[VMEM] * 3,
        compiler_params=pltpu.CompilerParams(vmem_limit_bytes=SCRATCH_BYTES),
        name="first_merge",
    )(*near_core(arrays))


def upper_merge(level, levels, arrays, buffer, pieces):
    size = arrays[1].shape[1]
    is_last = level == levels
    extra = [] if buffer is None else [buffer]
    out_shape = [jax.ShapeDtypeStruct((levels - 1, size, size), F32)]
    out_shape += [] if is_last else state_shapes(size, pieces)
    return pl.pallas_call(
        functools.partial(upper_kernel, level, is_last, bool(extra), (len(arrays) - 3) // 2),
        out_shape=out_shape,
        in_specs=[VMEM] * len(arrays) + [ANY] * len(extra),
        out_specs=[ANY] + [VMEM] * (len(out_shape) - 1),
        scratch_shapes=[pltpu.VMEM((size, size), F32), pltpu.SemaphoreType.DMA(())],
        input_output_aliases={len(arrays): 0} if extra else {},
        compiler_params=pltpu.CompilerParams(vmem_limit_bytes=SCRATCH_BYTES),
    )(*near_core(arrays), *extra)


def load_kernel(keys, place, mask, front, own, rows, own_here, arrived):
    slots, leaf = rows.shape[:2]
    own_copy = pltpu.make_async_copy(own, own_here, arrived.at[slots, 0])
    own_copy.start()
    tiles = []
    for slot in range(slots):
        for j, key in enumerate(keys):
            tile_row, chunk = place[1] ^ slot, place[0] ^ key
            row_tile = place[0] * slots + tile_row
            col_tile = place[1] * len(keys) + chunk
            present = (mask[tile_row, chunk] != 0) & (row_tile // 2 != col_tile // 2)
            here = rows.at[slot, :, pl.ds(j * leaf, leaf)]
            copy = pltpu.make_async_copy(
                front.at[
                    pl.ds(pl.multiple_of(tile_row * leaf, leaf), leaf),
                    pl.ds(pl.multiple_of(chunk * leaf, leaf), leaf),
                ],
                here,
                arrived.at[slot, j],
            )
            tiles.append((present, copy))

            @pl.when(present)
            def _():
                copy.start()

            @pl.when(jnp.logical_not(present))
            def _():
                here[...] = jnp.zeros(here.shape, BF16)

    for present, copy in tiles:

        @pl.when(present)
        def _():
            copy.wait()

    own_copy.wait()


def load_front(front, tile_mask, place, own, keys):
    leaf, size = own.shape
    slots, width = front.shape[0] // leaf, front.shape[1]
    small = width * size < 2**20
    form = pltpu.VMEM if small else jax.ShapeDtypeStruct
    return pl.pallas_call(
        functools.partial(load_kernel, keys),
        out_shape=[form((slots, leaf, width), BF16), form((leaf, size), BF16)],
        in_specs=[SMEM, SMEM, ANY, ANY],
        out_specs=[VMEM] * 2,
        scratch_shapes=[pltpu.SemaphoreType.DMA((slots + 1, len(keys)))],
        compiler_params=pltpu.CompilerParams(vmem_limit_bytes=SCRATCH_BYTES * (1 if small else 3)),
        name="load_front",
    )(
        place,
        tile_mask,
        pltpu.with_memory_space_constraint(front, pltpu.HBM),
        pltpu.with_memory_space_constraint(own, pltpu.HBM),
    )


def sample_kernel(rows, *refs):
    chunks, (keep, send) = refs[:-2], refs[-2:]
    slots = rows.shape[0]
    probes = jnp.concatenate([x[...] for x in chunks], axis=0)
    for slot in [*range(1, slots, 2), *range(0, slots, 2)]:
        out = send if slot % 2 else keep
        out[slot // 2] = dot(rows[slot], probes, (1, 0))


def all_samples(rows, chunks):
    slots, leaf, width = rows.shape
    size = chunks[0].shape[1]
    small = width * size < 2**20
    form = pltpu.VMEM if small else jax.ShapeDtypeStruct
    arrays = [rows, *chunks]
    return pl.pallas_call(
        sample_kernel,
        out_shape=[form((slots // 2, leaf, size), F32)] * 2,
        in_specs=[VMEM] * len(arrays),
        out_specs=[VMEM] * 2,
        compiler_params=pltpu.CompilerParams(vmem_limit_bytes=SCRATCH_BYTES * (1 if small else 3)),
        name="samples",
    )(*(near_core(arrays) if small else arrays))


def swap(x, axis, bit):
    return lax.ppermute(x, axis, [(i, i ^ (1 << bit)) for i in range(lax.axis_size(axis))])


def step(front, tile_mask, probes, coupling):
    col_count, row_count = lax.axis_size("col"), lax.axis_size("row")
    row_index, col_index = lax.axis_index("row"), lax.axis_index("col")
    col_levels, row_levels = col_count.bit_length() - 1, row_count.bit_length() - 1
    levels = col_levels + row_levels
    place = jnp.stack([row_index, col_index]).astype(jnp.int32)
    bits = [("col", b) for b in range(col_levels)] + [("row", b) for b in range(row_levels)]

    chunks = {0: probes}
    chunks[1] = swap(probes, "row", 0)
    for bit in range(row_levels - 1, 0, -1):
        for key in list(chunks):
            new = key | 1 << bit
            if key == 1:
                chunks[new] = swap(chunks[new ^ 1], "row", 0)
            else:
                chunks[new] = swap(chunks[key], "row", bit)

    home = [((b % row_count) * col_count + b // row_count, b) for b in range(row_count * col_count)]
    own_w = lax.ppermute(probes, ("row", "col"), home)
    other_w = swap(own_w, "col", 0)

    own_p, other_p, total_p = {}, {}, coupling
    for level, (axis, bit) in enumerate(bits, start=1):
        own_p[level], other_p[level] = total_p, swap(total_p, axis, bit)
        if level < levels:
            total_p = own_p[level] + other_p[level]

    order = list(chunks)
    rows, own_chunk = load_front(front, tile_mask, place, probes, order)
    keep, send = all_samples(rows, [own_chunk] + [chunks[k] for k in order[1:]])
    got = swap(send, "col", 0)
    slots = {2 * k: (keep[k], got[k]) for k in range(col_count // 2)}
    for bit in range(1, col_levels):
        far = 1 << bit
        left = list(range(0, col_count, 2 * far))
        moved = swap(jnp.stack([slots[k + far][0] + slots[k + far][1] for k in left]), "col", bit)
        slots = {k: (slots[k][0] + slots[k][1], moved[i]) for i, k in enumerate(left)}
    own_a, own_b = slots[0]
    other_a = swap(own_a, "col", 0)
    other_b = swap(own_b, "col", 0)

    def pieces(level):
        return 2 if level == levels and col_levels > 1 and row_levels > 0 else 1

    leaf_basis, state, send = first_merge(
        (own_a, own_b, other_a, other_b, own_w, other_w), pieces(2)
    )
    buffer = None
    for level, (axis, bit) in list(enumerate(bits, start=1))[1:]:
        near = [swap(send, axis, bit)]
        if pieces(level) > 1:
            near.append(swap(near[0], "col", 1))
        far = []
        for x in near:
            far.append(swap(x, "col", 0))
        buffer, *rest = upper_merge(
            level,
            levels,
            (state, own_p[level], other_p[level], *near, *far),
            buffer,
            pieces(level + 1),
        )
        if rest:
            state, send = rest
    return (leaf_basis, buffer)


def solution(mesh):
    in_specs = (P("row", "col"), P("row", "col"), P(("col", "row"), None), P(("row", "col"), None))
    out_specs = (P(("row", "col"), None), P(None, ("row", "col"), None))
    return jax.shard_map(step, mesh=mesh, in_specs=in_specs, out_specs=out_specs, check_vma=False)
```

```python
import functools

import jax
import jax.numpy as jnp
from jax import lax
from jax.experimental import pallas as pl
from jax.experimental.pallas import tpu as pltpu
from jax.sharding import PartitionSpec as P

F32 = jnp.float32
BF16 = jnp.bfloat16
SUB, LANE = 8, 128
BLOCK = LANE // 2
PANEL = 2
SCRATCH_BYTES = 16 * 2**20


def split(x):
    high = x.astype(BF16)
    return high, (x - high.astype(F32)).astype(BF16)


def dot(left, right, dims):
    return lax.dot_general(
        left, right, (((dims[0],), (dims[1],)), ((), ())), preferred_element_type=F32
    )


def product(left, right, dims):
    total = None
    for i in reversed(range(len(left))):
        for j in reversed(range(len(right))):
            if i + j < 2:
                term = dot(left[i], right[j], dims)
                total = term if total is None else total + term
    return total


def lane_copy(x, lane):
    return jnp.take_along_axis(
        x, jnp.full(x.shape, lane, jnp.int32), axis=1, mode="promise_in_bounds"
    )


def row_copy(x, row):
    return jnp.broadcast_to(x[row : row + 1, :], x.shape)


def tree_sum(terms):
    while len(terms) > 1:
        pairs = [terms[i] + terms[i + 1] for i in range(0, len(terms) - 1, 2)]
        terms = pairs + terms[len(pairs) * 2 :]
    return terms[0]


def factor_block(packed, offset):
    count = BLOCK // SUB
    rows = [packed[SUB * k : SUB * (k + 1), :] for k in range(count)]
    sub = lax.broadcasted_iota(jnp.int32, (SUB, LANE), 0)
    out = []
    for first in range(0, count, PANEL):
        width, start = SUB * PANEL, offset + SUB * first
        held = rows[first : first + PANEL]
        cols = [[lane_copy(held[q], start + t) for q in range(PANEL)] for t in range(width)]
        done, scales = [None] * PANEL, [None] * PANEL
        for s in range(width):
            own, at = divmod(s, SUB)
            if at == 0:
                for t in range(s, width):
                    for q in range(own):
                        cols[t][q] = lane_copy(held[q], start + t)
            here = sub == at
            pivot = row_copy(cols[s][own], at)
            scale = 1.0 / pivot
            root = lax.rsqrt(pivot)
            bare = [jnp.where(here, 0.0, cols[s][q]) if q == own else cols[s][q] for q in range(PANEL)]
            factor = [x * scale for x in bare]
            row = row_copy(held[own], at)
            if at == 0:
                done[own], scales[own] = row * root, scale
            else:
                done[own] = jnp.where(here, row * root, done[own])
                scales[own] = jnp.where(here, scale, scales[own])
            for t in range(s + 1, width):
                across = row_copy(cols[s][t // SUB], t % SUB)
                for q in range(PANEL):
                    if q < t // SUB and own < t // SUB:
                        continue
                    if t == s + 1:
                        cols[t][q] = cols[t][q] - (bare[q] * across) * scale
                    else:
                        cols[t][q] = cols[t][q] - factor[q] * across
            for q in range(PANEL):
                held[q] = held[q] - factor[q] * row
        out += done
        if first + PANEL < count:
            held = [held[q] * scales[q] for q in range(PANEL)]
            solved = [row_copy(held[s // SUB], s % SUB) for s in range(width)]
            for k in range(first + PANEL, count):
                weight = [lane_copy(rows[k], start + s) for s in range(width)]
                rows[k] = rows[k] - tree_sum([weight[s] * solved[s] for s in range(width)])
    return jnp.concatenate(out, axis=0)


def four(x):
    high, low = split(x)
    return jnp.concatenate([high, high, low, low], axis=0)


def two_parts(x):
    high = x.astype(BF16).astype(F32)
    return high, x - high


def factor_all(gram, rights):
    count = gram.shape[0] // BLOCK
    lane = lax.broadcasted_iota(jnp.int32, (BLOCK, LANE), 1)
    sub = lax.broadcasted_iota(jnp.int32, (BLOCK, LANE), 0)
    blocks = [gram[BLOCK * i : BLOCK * (i + 1), :] for i in range(count)]
    rights = [[x[BLOCK * i : BLOCK * (i + 1), :] for i in range(count)] for x in rights]
    upper, solved = [], [[] for _ in rights]
    for i in range(count):
        first, offset = BLOCK * i // LANE * LANE, BLOCK * i % LANE
        other = BLOCK - offset
        mine = (lane >= offset) & (lane < offset + BLOCK)
        tile = slice(first, first + LANE)
        both = factor_block(
            jnp.where(mine, blocks[i][:, tile], jnp.where(lane - other == sub, 1.0, 0.0)), offset
        )
        high, low = two_parts(jnp.where(mine, 0.0, both))
        low_here = pltpu.roll(low, BLOCK, 1)
        left = jnp.concatenate([jnp.where(mine, low_here, high), high], axis=1).astype(BF16)
        row = both
        if i + 1 < count:
            row = dot(left, four(blocks[i][:, first:]), (1, 0))
            high_here = pltpu.roll(high, BLOCK, 1)
            across = jnp.concatenate([high_here, low_here, high_here], axis=1).astype(BF16)
            below = jnp.concatenate([blocks[j][:, tile] for j in range(i + 1, count)], axis=0)
            high, low = split(below)
            column = dot(
                jnp.concatenate([high, high, low], axis=1),
                jnp.concatenate([across, across], axis=0),
                (1, 1),
            )
            high, low = two_parts(column)
            near = lax.broadcasted_iota(jnp.int32, column.shape, 1) < BLOCK
            column = jnp.concatenate(
                [jnp.where(near, high, low), jnp.where(near, high, 0.0)], axis=1
            ).astype(BF16)
            change = dot(column, four(row), (1, 0))
            for j in range(i + 1, count):
                at = BLOCK * (j - i - 1)
                new = blocks[j][:, first:] - change[at : at + BLOCK, :]
                if first:
                    new = jnp.concatenate([blocks[j][:, :first], new], axis=1)
                blocks[j] = new
        for x, y in zip(rights, solved):
            y.append(dot(left, four(x[i]), (1, 0)))
            if i + 1 < count:
                change = dot(column, four(y[i]), (1, 0))
                for j in range(i + 1, count):
                    at = BLOCK * (j - i - 1)
                    x[j] = x[j] - change[at : at + BLOCK, :]
        head = jnp.where(mine, both, row[:, :LANE])
        head = jnp.where(lane < offset + jnp.where(mine, sub, 0), 0.0, head)
        upper.append(head if row.shape[1] == LANE else jnp.concatenate([head, row[:, LANE:]], axis=1))
    return upper, [jnp.concatenate(x, axis=0) for x in solved]


def merge_math(own, other, level, want_state):
    own_s, own_w, own_p = own
    other_s, other_w, other_p = other
    if level > 1:
        factor = 2.0 ** (-(level - 1) / 2.0)
        own_s = own_s - factor * product(own_p, other_w, (1, 0))
        other_s = other_s - factor * product(other_p, own_w, (1, 0))
    size = own_s.shape[1]
    own_h, other_h = split(own_s), split(other_s)
    gram = product(own_h, own_h, (0, 0)) + product(other_h, other_h, (0, 0))
    trace = jnp.sum(own_s * own_s) + jnp.sum(other_s * other_s)
    shift = 0.001 * (trace / size + 1e-06)
    eye = lax.broadcasted_iota(jnp.int32, (size, size), 0) == lax.broadcasted_iota(
        jnp.int32, (size, size), 1
    )
    rights = [jnp.where(eye, 1.0, 0.0)]
    if want_state:
        rights.append(product(own_h, own_w, (0, 0)) + product(other_h, other_w, (0, 0)))
    upper, solved = factor_all(gram + jnp.where(eye, shift, 0.0), rights)
    q = product(own_h, split(solved[0]), (1, 1))
    return q, upper, solved[1] if want_state else None


def store_state(side, upper, w, state, send):
    half = w.shape[0] // 2
    part = half // 2
    share = half - part // 2
    state[0, :half] = w[:half]
    state[1, :half] = w[half:]
    top = jnp.concatenate(upper[:2], axis=0)
    state[0, half:] = top[:share]
    state[1, half : half + half - share] = top[share:]
    state[1, half + half - share :] = jnp.concatenate(upper[2:], axis=1)
    rows = send.shape[0]
    if rows == state.shape[1]:
        send[...] = state[side[0]]
    else:
        send[...] = state[side[0], pl.ds(pl.multiple_of(side[1] * rows, SUB), rows)]


def load_state(first, second):
    half = first.shape[1] // 2
    part = half // 2
    share = half - part // 2
    w = jnp.concatenate([first[:half], second[:half]], axis=0)
    split_at = half + half - share
    top = jnp.concatenate([first[half:], second[half:split_at]], axis=0)
    last = second[split_at:]
    corner = jnp.concatenate([last[:, :half], last[:, half:]], axis=0)
    bottom = jnp.concatenate([jnp.zeros((half, half), F32), corner], axis=1)
    return jnp.concatenate([top, bottom], axis=0), w


def chip_side():
    col = lax.axis_index("col")
    return col & 1, col >> 1 & 1


def first_kernel(
    own_a, own_b, other_a, other_b, own_w, other_w, q_out, state, send
):
    q, upper, w = merge_math(
        (own_a[...] + own_b[...], (own_w[...],), None),
        (other_a[...] + other_b[...], (other_w[...],), None),
        1,
        True,
    )
    store_state(chip_side(), upper, w, state, send)
    q_out[...] = q


def gather_half(side, pieces):
    if len(pieces) == 1:
        return pieces[0][...]
    mine, theirs = pieces[0][...], pieces[1][...]
    is_first = side[1] == 0
    return jnp.concatenate(
        [jnp.where(is_first, mine, theirs), jnp.where(is_first, theirs, mine)], axis=0
    )


def upper_kernel(level, is_last, has_earlier, has_buffer, pieces, own, own_p, other_p, *refs):
    side = chip_side()
    near, far, refs = list(refs[:pieces]), list(refs[pieces : 2 * pieces]), list(refs[2 * pieces :])
    earlier = refs.pop(0) if has_earlier else None
    if has_buffer:
        refs.pop(0)
    q_all = refs.pop(0) if has_earlier or is_last else None
    q_here, *outs = refs[:-1]
    done = refs[-1]
    if has_earlier:
        early = pltpu.make_async_copy(earlier, q_all.at[level - 3], done.at[0])
        early.start()
    is_first = side[0] == 0
    own_s, own_w = load_state(own[0], own[1])
    near, far = gather_half(side, near), gather_half(side, far)
    other_s, other_w = load_state(jnp.where(is_first, near, far), jnp.where(is_first, far, near))
    q, upper, w = merge_math(
        (own_s, split(own_w), split(own_p[...])),
        (other_s, split(other_w), split(other_p[...])),
        level,
        not is_last,
    )
    q_here[...] = q
    if is_last:
        late = pltpu.make_async_copy(q_here, q_all.at[level - 2], done.at[1])
        late.start()
        late.wait()
    else:
        store_state(side, upper, w, *outs)
    if has_earlier:
        early.wait()


VMEM = pl.BlockSpec(memory_space=pltpu.VMEM)
SMEM = pl.BlockSpec(memory_space=pltpu.SMEM)
ANY = pl.BlockSpec(memory_space=pl.ANY)


def near_core(arrays):
    return [pltpu.with_memory_space_constraint(x, pltpu.VMEM) for x in arrays]


def state_shapes(size, pieces):
    rows = size // 2 + 3 * size // 8
    return [pltpu.VMEM((2, rows, size), F32), pltpu.VMEM((rows // pieces, size), F32)]


def first_merge(arrays, pieces):
    rows, size = arrays[0].shape
    return pl.pallas_call(
        first_kernel,
        out_shape=[jax.ShapeDtypeStruct((rows, size), F32)] + state_shapes(size, pieces),
        in_specs=[VMEM] * len(arrays),
        out_specs=[VMEM] * 3,
        compiler_params=pltpu.CompilerParams(vmem_limit_bytes=SCRATCH_BYTES),
        name="first_merge",
    )(*near_core(arrays))


def upper_merge(level, levels, arrays, earlier, buffer, pieces):
    size = arrays[1].shape[1]
    is_last = level == levels
    held = list(arrays) + ([] if earlier is None else [earlier])
    extra = [] if buffer is None else [buffer]
    out_shape, out_specs = [], []
    if is_last or earlier is not None:
        out_shape.append(jax.ShapeDtypeStruct((levels - 1, size, size), F32))
        out_specs.append(ANY)
    here = pltpu.VMEM((size, size), F32)
    if not is_last:
        more = [here] + state_shapes(size, pieces)
        out_shape += more
        out_specs += [VMEM] * len(more)
    results = pl.pallas_call(
        functools.partial(
            upper_kernel, level, is_last, earlier is not None, bool(extra), (len(arrays) - 3) // 2
        ),
        out_shape=out_shape,
        in_specs=[VMEM] * len(held) + [ANY] * len(extra),
        out_specs=out_specs,
        scratch_shapes=([here] if is_last else []) + [pltpu.SemaphoreType.DMA((2,))],
        input_output_aliases={len(held): 0} if extra else {},
        compiler_params=pltpu.CompilerParams(vmem_limit_bytes=SCRATCH_BYTES),
    )(*near_core(held), *extra)
    if is_last:
        return results[0], None, None, None
    return (None, *results) if earlier is None else tuple(results)


def load_kernel(keys, place, mask, front, own, rows, own_here, arrived):
    slots, leaf = rows.shape[:2]
    own_copy = pltpu.make_async_copy(own, own_here, arrived.at[slots, 0])
    own_copy.start()
    tiles = []
    for slot in range(slots):
        for j, key in enumerate(keys):
            tile_row, chunk = place[1] ^ slot, place[0] ^ key
            row_tile = place[0] * slots + tile_row
            col_tile = place[1] * len(keys) + chunk
            present = (mask[tile_row, chunk] != 0) & (row_tile // 2 != col_tile // 2)
            here = rows.at[slot, :, pl.ds(j * leaf, leaf)]
            copy = pltpu.make_async_copy(
                front.at[
                    pl.ds(pl.multiple_of(tile_row * leaf, leaf), leaf),
                    pl.ds(pl.multiple_of(chunk * leaf, leaf), leaf),
                ],
                here,
                arrived.at[slot, j],
            )
            tiles.append((present, copy))

            @pl.when(present)
            def _():
                copy.start()

            @pl.when(jnp.logical_not(present))
            def _():
                here[...] = jnp.zeros(here.shape, BF16)

    for present, copy in tiles:

        @pl.when(present)
        def _():
            copy.wait()

    own_copy.wait()


def load_front(front, tile_mask, place, own, keys):
    leaf, size = own.shape
    slots, width = front.shape[0] // leaf, front.shape[1]
    small = width * size < 2**20
    form = pltpu.VMEM if small else jax.ShapeDtypeStruct
    return pl.pallas_call(
        functools.partial(load_kernel, keys),
        out_shape=[form((slots, leaf, width), BF16), form((leaf, size), BF16)],
        in_specs=[SMEM, SMEM, ANY, ANY],
        out_specs=[VMEM] * 2,
        scratch_shapes=[pltpu.SemaphoreType.DMA((slots + 1, len(keys)))],
        compiler_params=pltpu.CompilerParams(vmem_limit_bytes=SCRATCH_BYTES * (1 if small else 3)),
        name="load_front",
    )(
        place,
        tile_mask,
        pltpu.with_memory_space_constraint(front, pltpu.HBM),
        pltpu.with_memory_space_constraint(own, pltpu.HBM),
    )


def sample_kernel(rows, *refs):
    chunks, (keep, send) = refs[:-2], refs[-2:]
    slots = rows.shape[0]
    probes = jnp.concatenate([x[...] for x in chunks], axis=0)
    for slot in [*range(1, slots, 2), *range(0, slots, 2)]:
        out = send if slot % 2 else keep
        out[slot // 2] = dot(rows[slot], probes, (1, 0))


def all_samples(rows, chunks):
    slots, leaf, width = rows.shape
    size = chunks[0].shape[1]
    small = width * size < 2**20
    form = pltpu.VMEM if small else jax.ShapeDtypeStruct
    arrays = [rows, *chunks]
    return pl.pallas_call(
        sample_kernel,
        out_shape=[form((slots // 2, leaf, size), F32)] * 2,
        in_specs=[VMEM] * len(arrays),
        out_specs=[VMEM] * 2,
        compiler_params=pltpu.CompilerParams(vmem_limit_bytes=SCRATCH_BYTES * (1 if small else 3)),
        name="samples",
    )(*(near_core(arrays) if small else arrays))


def swap(x, axis, bit):
    return lax.ppermute(x, axis, [(i, i ^ (1 << bit)) for i in range(lax.axis_size(axis))])


def step(front, tile_mask, probes, coupling):
    col_count, row_count = lax.axis_size("col"), lax.axis_size("row")
    row_index, col_index = lax.axis_index("row"), lax.axis_index("col")
    col_levels, row_levels = col_count.bit_length() - 1, row_count.bit_length() - 1
    levels = col_levels + row_levels
    place = jnp.stack([row_index, col_index]).astype(jnp.int32)
    bits = [("col", b) for b in range(col_levels)] + [("row", b) for b in range(row_levels)]

    chunks = {0: probes}
    chunks[1] = swap(probes, "row", 0)
    for bit in range(row_levels - 1, 0, -1):
        for key in list(chunks):
            new = key | 1 << bit
            if key == 1:
                chunks[new] = swap(chunks[new ^ 1], "row", 0)
            else:
                chunks[new] = swap(chunks[key], "row", bit)

    home = [((b % row_count) * col_count + b // row_count, b) for b in range(row_count * col_count)]
    own_w = lax.ppermute(probes, ("row", "col"), home)
    other_w = swap(own_w, "col", 0)

    own_p, other_p, total_p = {}, {}, coupling
    for level, (axis, bit) in enumerate(bits, start=1):
        own_p[level], other_p[level] = total_p, swap(total_p, axis, bit)
        if level < levels:
            total_p = own_p[level] + other_p[level]

    order = list(chunks)
    rows, own_chunk = load_front(front, tile_mask, place, probes, order)
    keep, send = all_samples(rows, [own_chunk] + [chunks[k] for k in order[1:]])
    got = swap(send, "col", 0)
    slots = {2 * k: (keep[k], got[k]) for k in range(col_count // 2)}
    for bit in range(1, col_levels):
        far = 1 << bit
        left = list(range(0, col_count, 2 * far))
        moved = swap(jnp.stack([slots[k + far][0] + slots[k + far][1] for k in left]), "col", bit)
        slots = {k: (slots[k][0] + slots[k][1], moved[i]) for i, k in enumerate(left)}
    own_a, own_b = slots[0]
    other_a = swap(own_a, "col", 0)
    other_b = swap(own_b, "col", 0)

    def pieces(level):
        return 2 if level == levels and col_levels > 1 and row_levels > 0 else 1

    leaf_basis, state, send = first_merge(
        (own_a, own_b, other_a, other_b, own_w, other_w), pieces(2)
    )
    buffer = earlier = None
    for level, (axis, bit) in list(enumerate(bits, start=1))[1:]:
        near = [swap(send, axis, bit)]
        if pieces(level) > 1:
            near.append(swap(near[0], "col", 1))
        far = []
        for x in near:
            far.append(swap(x, "col", 0))
        buffer, earlier, state, send = upper_merge(
            level,
            levels,
            (state, own_p[level], other_p[level], *near, *far),
            earlier,
            buffer,
            pieces(level + 1),
        )
    return (leaf_basis, buffer)


def solution(mesh):
    in_specs = (P("row", "col"), P("row", "col"), P(("col", "row"), None), P(("row", "col"), None))
    out_specs = (P(("row", "col"), None), P(None, ("row", "col"), None))
    return jax.shard_map(step, mesh=mesh, in_specs=in_specs, out_specs=out_specs, check_vma=False)
```
